32 devices in a mesh: dp: 8 (over y, x, core), mp: 4 (over z).
Axes of the slice: x: 2, y: 2, z: 4, core: 2. Of those that a mesh axis runs over, the one named last changes fastest.
Arguments:
- tokens: bfloat16 [16384, 2048], P(('dp', 'mp')), may hold values from -6 to 6
- lengths: int32 [8], P('dp'), may hold values from 128 to 2048, as said below
- cotangent: bfloat16 [16384, 2048], P(('dp', 'mp')), may hold values from -6 to 6
- first_gain: float32 [2048], replicated, may hold values from 0.25 to 1.75
- first_shift: float32 [2048], replicated, may hold values from -4 to 4
- second_gain: float32 [2048], replicated, may hold values from 0.25 to 1.75
- second_shift: float32 [2048], replicated, may hold values from -4 to 4
- attend_weight: bfloat16 [3, 2048, 2048], P(None, None, 'mp'), may hold values from -0.125 to 0.125
- attend_bias: float32 [3, 2048], P(None, 'mp'), may hold values from -6 to 6
- merge_weight: bfloat16 [2048, 2048], P('mp'), may hold values from -0.5 to 0.5
- merge_bias: float32 [2048], replicated, may hold values from -4 to 4
- expand_weight: bfloat16 [2048, 8192], P(None, 'mp'), may hold values from -0.125 to 0.125
- expand_bias: float32 [8192], P('mp'), may hold values from -6 to 6
- contract_weight: bfloat16 [8192, 2048], P('mp'), may hold values from -0.0625 to 0.0625
- contract_bias: float32 [2048], replicated, may hold values from -4 to 4
Outputs:
- layer_output: bfloat16 [16384, 2048], P(('dp', 'mp'))
- tokens_grad: bfloat16 [16384, 2048], P(('dp', 'mp'))
- first_gain_grad: float32 [2048], replicated
- first_shift_grad: float32 [2048], replicated
- second_gain_grad: float32 [2048], replicated
- second_shift_grad: float32 [2048], replicated
- attend_weight_grad: float32 [3, 2048, 2048], P(None, None, 'mp')
- attend_bias_grad: float32 [3, 2048], P(None, 'mp')
- merge_weight_grad: float32 [2048, 2048], P('mp')
- merge_bias_grad: float32 [2048], replicated
- expand_weight_grad: float32 [2048, 8192], P(None, 'mp')
- expand_bias_grad: float32 [8192], P('mp')
- contract_weight_grad: float32 [8192, 2048], P('mp')
- contract_bias_grad: float32 [2048], replicated
The draws below stay inside these ranges and needn't reach their ends.
Inputs may be any that keep to these rules, and one draw needn't show every extreme that they name: Sequence b holds lengths[b] real tokens followed by padding; some sequence has 2048.
All inputs are finite; a program needn't handle non-finite values.
Results may differ from the reference program's by a relative error of at most 0.011.
Values may be sent and summed in bfloat16 or wider, within the bound.
No kernel may reach another device: no remote copies, remote signals or barrier semaphores. Data moves between devices by JAX's collectives and lax.ppermute only.
A program may use at most 320 MiB of HBM per device.

```python
import jax
import jax.numpy as jnp
from jax import lax

D = 2048
HEADS = 8
HD = 256
ROT = 64
FF = 8192
SEQ_LEN = 2048
SEQUENCES = 8
TOKENS = 16384


def draw_lengths(key, part):
    first_key, second_key = jax.random.split(key)
    drawn = jax.random.randint(first_key, (SEQUENCES,), SEQ_LEN // 16, SEQ_LEN + 1)
    longest = jax.random.randint(second_key, (), 0, SEQUENCES)
    return jnp.where(jnp.arange(SEQUENCES) == longest, SEQ_LEN, drawn).astype(jnp.int32)


def shard_levels(own_key, shape, cuts, smallest, top_value):
    loudness, own = 1.0, jax.random.fold_in(own_key, 6)
    for axis_at, shards_of in cuts:
        heights = jnp.exp(jax.random.uniform(jax.random.fold_in(own, axis_at), (shards_of,), jnp.float32, smallest / len(cuts), top_value / len(cuts)))
        loudness = loudness * jnp.repeat(heights, shape[axis_at] // shards_of).reshape([-1 if axis == axis_at else 1 for axis in range(len(shape))])
    return loudness


def scatter_about(own_key, extent, spread, limit, shards=(), held_as=jnp.bfloat16):
    factor_of = shard_levels(own_key, extent, shards, -0.22, 0.18) if shards else 1.0
    values = jax.random.normal(own_key, extent, jnp.float32) * spread * factor_of
    return jnp.minimum(jnp.maximum(values, -limit), limit).astype(held_as)


def setup_inputs(seed: int = 0) -> dict:
    key_of = jax.random.split(jax.random.key(seed), 16)
    return {
        "tokens": scatter_about(key_of[0], (TOKENS, D), 1.0, 6.0, ((0, 32),)),
        "lengths": draw_lengths(jax.random.fold_in(key_of[15], 71), 0),
        "cotangent": scatter_about(key_of[2], (TOKENS, D), 1.0, 6.0, ((0, 32),)),
        "first_gain": jnp.clip(1.0 + 0.15 * jax.random.normal(key_of[3], (D,), jnp.float32), 0.25, 1.75),
        "first_shift": scatter_about(key_of[4], (D,), 0.3, 4.0, (), jnp.float32),
        "second_gain": jnp.clip(1.0 + 0.15 * jax.random.normal(key_of[5], (D,), jnp.float32), 0.25, 1.75),
        "second_shift": scatter_about(key_of[6], (D,), 0.3, 4.0, (), jnp.float32),
        "attend_weight": scatter_about(key_of[7], (3, D, D), D ** -0.5, 0.125, ((2, 4),)),
        "attend_bias": scatter_about(key_of[8], (3, D), 0.5, 6.0, ((1, 4),), jnp.float32),
        "merge_weight": scatter_about(key_of[9], (D, D), (D // 16) ** -0.5, 0.5, ((0, 4),)),
        "merge_bias": scatter_about(key_of[10], (D,), 0.3, 4.0, (), jnp.float32),
        "expand_weight": scatter_about(key_of[11], (D, FF), D ** -0.5, 0.125, ((1, 4),)),
        "expand_bias": scatter_about(key_of[12], (FF,), 0.5, 6.0, ((0, 4),), jnp.float32),
        "contract_weight": scatter_about(key_of[13], (FF, D), FF ** -0.5, 0.0625, ((0, 4),)),
        "contract_bias": scatter_about(key_of[14], (D,), 0.3, 4.0, (), jnp.float32),
    }


@jax.custom_vjp
def low(v):
    return lax.optimization_barrier(v.astype(jnp.bfloat16)).astype(jnp.float32)

@jax.custom_vjp
def low_back(v):
    return v

def low_keep(v):
    return (low(v), None)

def low_pass(kept, grad):
    return (grad,)

def back_keep(v):
    return (v, None)

def back_low(kept, grad):
    return (low(grad),)
low.defvjp(low_keep, low_pass)
low_back.defvjp(back_keep, back_low)
highest = lax.Precision.HIGHEST
norm_eps = 1e-05
masked_score = -1e+30

def layer_norm(inputs, gain_values, shift_values):
    average = lax.optimization_barrier(jnp.mean(inputs, axis=-1, keepdims=True))
    centred = inputs - average
    variance = lax.optimization_barrier(jnp.mean(centred * centred, axis=-1, keepdims=True))
    return centred * lax.rsqrt(variance + norm_eps) * gain_values + shift_values

def rotary_tables(length, rotated):
    halfway = rotated // 2
    channel = jnp.arange(halfway).astype(jnp.float32)
    frequency = 1.0 / 10000.0 ** (channel * 2.0 / rotated)
    positions = jnp.arange(length).astype(jnp.float32)
    angles = positions[:, None] * frequency[None, :]
    angles = jnp.concatenate([angles, angles], axis=1)
    return (jnp.cos(angles), jnp.sin(angles))

def rotate(per_head, cosine, sine_table, rotated):
    halfway = rotated // 2
    leading = per_head[..., :rotated]
    turned = jnp.concatenate([-leading[..., halfway:], leading[..., :halfway]], axis=-1)
    rotated_part = leading * cosine[:, None, :] + turned * sine_table[:, None, :]
    return jnp.concatenate([rotated_part, per_head[..., rotated:]], axis=-1)

def attention(queries, keys_all, values_all, seq_length):
    block_rows = min(512, SEQ_LEN)
    block_count = SEQ_LEN // block_rows
    key_places = jnp.arange(SEQ_LEN)

    def one_block(block_item):
        query_block, block_index = block_item
        query_places = block_index * block_rows + jnp.arange(block_rows)
        allowed = (key_places[None, :] <= query_places[:, None]) & (key_places[None, :] < seq_length)
        scores = low_back(jnp.einsum('qhd,khd->hqk', query_block, keys_all, precision=highest))
        scores = jnp.where(allowed[None], scores, masked_score)
        weights = low(jax.nn.softmax(scores, axis=-1))
        return jnp.einsum('hqk,khd->qhd', weights, values_all, precision=highest)
    blocked = queries.reshape(block_count, block_rows, HEADS, HD)
    outputs = lax.map(jax.checkpoint(one_block), (blocked, jnp.arange(block_count)))
    return outputs.reshape(SEQ_LEN, HEADS, HD)

def forward(params, inputs, seq_length, cosine, sine_table):
    first_gain, first_shift, second_gain, second_shift, attend_weight, attend_bias, merge_weight, merge_bias, expand_weight, expand_bias, contract_weight, contract_bias = params
    normed_one = low(layer_norm(inputs, first_gain, first_shift))
    normed_two = low(layer_norm(inputs, second_gain, second_shift))
    projected = jnp.einsum('td,cde->cte', normed_one, attend_weight, precision=highest)
    projected = low_back(projected + attend_bias[:, None, :])
    per_head = projected.reshape(3, SEQ_LEN, HEADS, HD)
    queries = low(rotate(per_head[0], cosine, sine_table, ROT) * HD ** (-0.5))
    keys_all = low(rotate(per_head[1], cosine, sine_table, ROT))
    values_all = low(per_head[2])
    attended = attention(queries, keys_all, values_all, seq_length)
    mixed = low_back(low(attended.reshape(SEQ_LEN, D)))
    hidden_pre = low_back(jnp.dot(normed_two, expand_weight, precision=highest) + expand_bias)
    activated = low_back(low(jax.nn.gelu(hidden_pre, approximate=False)))
    attn_branch = jnp.dot(mixed, merge_weight, precision=highest) + merge_bias
    feed_branch = jnp.dot(activated, contract_weight, precision=highest) + contract_bias
    return inputs + attn_branch + feed_branch

def reference(tokens, lengths, cotangent, first_gain, first_shift, second_gain, second_shift, attend_weight, attend_bias, merge_weight, merge_bias, expand_weight, expand_bias, contract_weight, contract_bias):
    params = (first_gain.astype(jnp.float32), first_shift.astype(jnp.float32), second_gain.astype(jnp.float32), second_shift.astype(jnp.float32), attend_weight.astype(jnp.float32), attend_bias.astype(jnp.float32), merge_weight.astype(jnp.float32), merge_bias.astype(jnp.float32), expand_weight.astype(jnp.float32), expand_bias.astype(jnp.float32), contract_weight.astype(jnp.float32), contract_bias.astype(jnp.float32))
    inputs = tokens.astype(jnp.float32).reshape(SEQUENCES, SEQ_LEN, D)
    places = jnp.arange(SEQ_LEN).astype(jnp.int32)
    valid_rows = places[None, :] < lengths[:, None]
    masked = jnp.where(valid_rows[:, :, None], cotangent.astype(jnp.float32).reshape(SEQUENCES, SEQ_LEN, D), jnp.float32(0.0))
    cosine, sine_table = rotary_tables(SEQ_LEN, ROT)

    def one_sequence(totals, seq_item):
        seq_rows, seq_cot, seq_length = seq_item
        result, pullback = jax.vjp(lambda weights, rows_in: forward(weights, rows_in, seq_length, cosine, sine_table), params, seq_rows)
        param_grads, input_grads = pullback(seq_cot)
        return (jax.tree.map(jnp.add, totals, param_grads), (result, input_grads))
    start_totals = jax.tree.map(jnp.zeros_like, params)
    totals, (results, input_grads) = lax.scan(one_sequence, start_totals, (inputs, masked, lengths))
    first_gain_grad, first_shift_grad, second_gain_grad, second_shift_grad, attend_weight_grad, attend_bias_grad, merge_weight_grad, merge_bias_grad, expand_weight_grad, expand_bias_grad, contract_weight_grad, contract_bias_grad = totals
    return (results.reshape(TOKENS, D).astype(jnp.bfloat16), input_grads.reshape(TOKENS, D).astype(jnp.bfloat16), first_gain_grad, first_shift_grad, second_gain_grad, second_shift_grad, attend_weight_grad, attend_bias_grad, merge_weight_grad, merge_bias_grad, expand_weight_grad, expand_bias_grad, contract_weight_grad, contract_bias_grad)
```

```python
from functools import partial

import jax
import jax.numpy as jnp
from jax import lax
from jax.experimental import pallas as pl
from jax.experimental.pallas import tpu as pltpu
from jax.sharding import PartitionSpec as P

HD = 256
ROT = 64
LANES = 128

norm_eps = 1e-05
masked_score = -1e30


def standardize(inputs):
    average = jnp.mean(inputs, axis=-1, keepdims=True)
    centred = inputs - average
    variance = jnp.mean(centred * centred, axis=-1, keepdims=True)
    inverse = lax.rsqrt(variance + norm_eps)
    return (centred * inverse, inverse)


def rotary_tables(length, rotated):
    halfway = rotated // 2
    channel = jnp.arange(halfway).astype(jnp.float32)
    frequency = 1.0 / 10000.0 ** (channel * 2.0 / rotated)
    positions = jnp.arange(length).astype(jnp.float32)
    angles = positions[:, None] * frequency[None, :]
    cosine, sine = jnp.cos(angles), jnp.sin(angles)
    rest = LANES - rotated
    ones, zeros = jnp.ones((length, rest), jnp.float32), jnp.zeros((length, rest), jnp.float32)
    none = jnp.zeros_like(sine)
    return (
        jnp.concatenate([cosine, cosine, ones], axis=1),
        jnp.concatenate([-sine, none, zeros], axis=1),
        jnp.concatenate([none, sine, zeros], axis=1),
    )


def turn_block(block, cosine, minus, plus, halfway):
    lead = block[:, :LANES]
    after = pltpu.roll(lead, LANES - halfway, 1)
    before = pltpu.roll(lead, halfway, 1)
    turned = lead * cosine + after * minus + before * plus
    return jnp.concatenate([turned, block[:, LANES:]], axis=1)


def forward_kernel(
    lengths, q_in, k_in, v_in, cos_q, min_q, plu_q, cos_k, min_k, plu_k,
    q_out, k_out, v_out, mixed_out, lse_out, *, rows, head_scale,
):
    step = pl.program_id(1)
    length = lengths[0]

    @pl.when(step == 0)
    def _():
        k_out[...] = turn_block(k_in[0], cos_k[...], min_k[...], plu_k[...], ROT // 2).astype(
            jnp.bfloat16
        )
        v_out[...] = v_in[0].astype(jnp.bfloat16)

    queries = (
        turn_block(q_in[0], cos_q[...], min_q[...], plu_q[...], ROT // 2) * head_scale
    ).astype(jnp.bfloat16)
    q_out[...] = queries

    def one_block(at, carried, diagonal):
        top, total, mixed = carried
        keys = k_out[pl.ds(at * rows, rows), :]
        values = v_out[pl.ds(at * rows, rows), :]
        scores = lax.dot_general(
            queries, keys, (((1,), (1,)), ((), ())), preferred_element_type=jnp.float32
        )
        places = lax.broadcasted_iota(jnp.int32, (rows, rows), 1)
        kept = places < length - at * rows
        if diagonal:
            kept = kept & (places <= lax.broadcasted_iota(jnp.int32, (rows, rows), 0))
        scores = jnp.where(kept, scores, masked_score)
        new_top = jnp.maximum(top, jnp.max(scores, axis=1, keepdims=True))
        shrink = jnp.exp(top - new_top)
        exponent = jnp.exp(scores - new_top)
        total = total * shrink + jnp.sum(exponent, axis=1, keepdims=True)
        mixed = mixed * shrink + lax.dot_general(
            exponent.astype(jnp.bfloat16),
            values,
            (((1,), (0,)), ((), ())),
            preferred_element_type=jnp.float32,
        )
        return (new_top, total, mixed)

    start = (
        jnp.full((rows, 1), masked_score, jnp.float32),
        jnp.zeros((rows, 1), jnp.float32),
        jnp.zeros((rows, HD), jnp.float32),
    )
    carried = lax.fori_loop(0, step, lambda at, c: one_block(at, c, False), start)
    top, total, mixed = one_block(step, carried, True)
    mixed_out[...] = (mixed / total).astype(jnp.bfloat16)
    lse_out[0] = top + jnp.log(total)


def backward_kernel(
    lengths, q_in, k_in, v_in, grad_in, mixed_in, lse_in, cosine, minus, plus,
    grads_out, key_sum, value_sum, *, rows, steps, head_scale,
):
    step = pl.program_id(1)
    length = lengths[0]

    @pl.when(step == 0)
    def _():
        key_sum[...] = jnp.zeros_like(key_sum)
        value_sum[...] = jnp.zeros_like(value_sum)

    queries = q_in[...]
    grads = grad_in[...]
    centre = jnp.sum(
        grads.astype(jnp.float32) * mixed_in[...].astype(jnp.float32), axis=1, keepdims=True
    )
    log_sum = lse_in[0]

    def one_block(at, grad_q, diagonal):
        span = pl.ds(at * rows, rows)
        keys = k_in[span, :]
        values = v_in[span, :]
        scores = lax.dot_general(
            queries, keys, (((1,), (1,)), ((), ())), preferred_element_type=jnp.float32
        )
        places = lax.broadcasted_iota(jnp.int32, (rows, rows), 1)
        kept = places < length - at * rows
        if diagonal:
            kept = kept & (places <= lax.broadcasted_iota(jnp.int32, (rows, rows), 0))
        weights = jnp.exp(jnp.where(kept, scores, masked_score) - log_sum)
        grad_w = lax.dot_general(
            grads, values, (((1,), (1,)), ((), ())), preferred_element_type=jnp.float32
        )
        grad_s = (weights * (grad_w - centre)).astype(jnp.bfloat16)
        key_sum[span, :] += lax.dot_general(
            grad_s, queries, (((0,), (0,)), ((), ())), preferred_element_type=jnp.float32
        )
        value_sum[span, :] += lax.dot_general(
            weights.astype(jnp.bfloat16),
            grads,
            (((0,), (0,)), ((), ())),
            preferred_element_type=jnp.float32,
        )
        return grad_q + lax.dot_general(
            grad_s, keys, (((1,), (0,)), ((), ())), preferred_element_type=jnp.float32
        )

    grad_q = lax.fori_loop(
        0, step, lambda at, c: one_block(at, c, False), jnp.zeros((rows, HD), jnp.float32)
    )
    grad_q = one_block(step, grad_q, True)
    here = pl.ds(step * rows, rows)
    grads_out[0, here, :] = (
        turn_block(grad_q, cosine[here, :], -minus[here, :], -plus[here, :], ROT // 2) * head_scale
    ).astype(jnp.bfloat16)

    @pl.when(step == steps - 1)
    def _():
        grads_out[1] = turn_block(
            key_sum[...], cosine[...], -minus[...], -plus[...], ROT // 2
        ).astype(jnp.bfloat16)
        grads_out[2] = value_sum[...].astype(jnp.bfloat16)


def attend_forward(projected, lengths, tables):
    _, span, width = projected.shape
    heads = width // HD
    rows = min(512, span)
    steps = span // rows
    low = jax.ShapeDtypeStruct((span, width), jnp.bfloat16)
    row_table = pl.BlockSpec((rows, LANES), lambda h, i, n: (i, 0))
    all_table = pl.BlockSpec((span, LANES), lambda h, i, n: (0, 0))
    row_block = pl.BlockSpec((rows, HD), lambda h, i, n: (i, h))
    all_block = pl.BlockSpec((span, HD), lambda h, i, n: (0, h))
    return pl.pallas_call(
        partial(forward_kernel, rows=rows, head_scale=HD ** (-0.5)),
        grid_spec=pltpu.PrefetchScalarGridSpec(
            num_scalar_prefetch=1,
            grid=(heads, steps),
            in_specs=[
                pl.BlockSpec((1, rows, HD), lambda h, i, n: (0, i, h)),
                pl.BlockSpec((1, span, HD), lambda h, i, n: (1, 0, h)),
                pl.BlockSpec((1, span, HD), lambda h, i, n: (2, 0, h)),
                row_table, row_table, row_table, all_table, all_table, all_table,
            ],
            out_specs=[
                row_block, all_block, all_block, row_block,
                pl.BlockSpec((1, rows, 1), lambda h, i, n: (h, i, 0)),
            ],
        ),
        out_shape=[low, low, low, low, jax.ShapeDtypeStruct((heads, span, 1), jnp.float32)],
        compiler_params=pltpu.CompilerParams(vmem_limit_bytes=48 * 1024 * 1024),
        name="attend_forward",
    )(lengths, projected, projected, projected, *tables, *tables)


def attend_backward(lengths, queries, keys, values, grad_mixed, mixed, lse, tables):
    span, width = queries.shape
    heads = width // HD
    rows = min(512, span)
    steps = span // rows
    all_table = pl.BlockSpec((span, LANES), lambda h, i, n: (0, 0))
    row_block = pl.BlockSpec((rows, HD), lambda h, i, n: (i, h))
    all_block = pl.BlockSpec((span, HD), lambda h, i, n: (0, h))
    return pl.pallas_call(
        partial(backward_kernel, rows=rows, steps=steps, head_scale=HD ** (-0.5)),
        grid_spec=pltpu.PrefetchScalarGridSpec(
            num_scalar_prefetch=1,
            grid=(heads, steps),
            in_specs=[
                row_block, all_block, all_block, row_block, row_block,
                pl.BlockSpec((1, rows, 1), lambda h, i, n: (h, i, 0)),
                all_table, all_table, all_table,
            ],
            out_specs=pl.BlockSpec((3, span, HD), lambda h, i, n: (0, 0, h)),
            scratch_shapes=[pltpu.VMEM((span, HD), jnp.float32)] * 2,
        ),
        out_shape=jax.ShapeDtypeStruct((3, span, width), jnp.bfloat16),
        compiler_params=pltpu.CompilerParams(vmem_limit_bytes=48 * 1024 * 1024),
        name="attend_backward",
    )(lengths, queries, keys, values, grad_mixed, mixed, lse, *tables)


def after(value, *others):
    return lax.optimization_barrier((value, *others))[0]


def on_device(
    tokens,
    lengths,
    cotangent,
    first_gain,
    first_shift,
    second_gain,
    second_shift,
    attend_weight,
    attend_bias,
    merge_weight,
    merge_bias,
    expand_weight,
    expand_bias,
    contract_weight,
    contract_bias,
):
    ring = lax.axis_size("mp")
    place = lax.axis_index("mp")
    rows_here, width = tokens.shape
    group_rows = rows_here * ring
    local_width = attend_weight.shape[2]
    local_hidden = expand_weight.shape[1]
    hops = [(i, (i + 1) % ring) for i in range(ring)]
    f32, bf16 = jnp.float32, jnp.bfloat16
    dot = partial(jnp.einsum, preferred_element_type=f32)

    def owner_row(s):
        return ((place - s) % ring) * rows_here

    def gather_ring(block):
        blocks = [block]
        for _ in range(ring - 1):
            block = lax.ppermute(block, "mp", hops)
            blocks.append(block)
        return blocks

    def in_order(blocks):
        whole = jnp.zeros((group_rows, blocks[0].shape[1]), blocks[0].dtype)
        for s, block in enumerate(blocks):
            whole = lax.dynamic_update_slice(whole, block, (owner_row(s), 0))
        return whole

    order = list(range(1, ring)) + [0]
    tables = rotary_tables(group_rows, ROT)

    token_blocks = gather_ring(tokens)
    row_ids = place * rows_here + jnp.arange(rows_here)
    valid_rows = row_ids < lengths[0]
    grad_out = jnp.where(valid_rows[:, None], cotangent, jnp.zeros_like(cotangent))
    grad_blocks = gather_ring(after(grad_out, token_blocks[-1]))

    projected = jnp.zeros((3, group_rows, local_width), f32)
    ones, twos, acts, slopes = [], [], [], []
    for s in range(ring):
        hat, _ = standardize(token_blocks[s].astype(f32))
        one = (hat * first_gain + first_shift).astype(bf16)
        two = (hat * second_gain + second_shift).astype(bf16)
        ones.append(one)
        twos.append(two)
        part = dot("td,cde->cte", one, attend_weight) + attend_bias[:, None, :]
        projected = lax.dynamic_update_slice(projected, part, (0, owner_row(s), 0))
        hidden = dot("td,df->tf", two, expand_weight) + expand_bias
        spread = 0.5 * (1.0 + lax.erf(hidden * (0.5**0.5)))
        bell = jnp.exp(-0.5 * hidden * hidden) * 0.3989422804014327
        acts.append((hidden * spread).astype(bf16))
        slopes.append((spread + hidden * bell).astype(bf16))

    queries, keys, values, mixed, lse = attend_forward(projected, lengths, tables)

    carried = None
    for s in order:
        mixed_rows = lax.dynamic_slice(mixed, (owner_row(s), 0), (rows_here, local_width))
        part = dot("tf,fd->td", mixed_rows, merge_weight)
        part = part + dot("tf,fd->td", acts[s], contract_weight)
        if carried is not None:
            part = part + carried.astype(f32)
        if s:
            send = part.astype(bf16)
            if carried is None:
                send = after(send, grad_blocks[-1])
            carried = lax.ppermute(send, "mp", hops)
    layer_output = (tokens.astype(f32) + part + merge_bias + contract_bias).astype(bf16)

    hidden_grads = []
    grad_mixed = jnp.zeros((group_rows, local_width), bf16)
    for s in range(ring):
        grad_act = dot("td,fd->tf", grad_blocks[s], contract_weight)
        hidden_grads.append((grad_act * slopes[s].astype(f32)).astype(bf16))
        rows = dot("td,fd->tf", grad_blocks[s], merge_weight).astype(bf16)
        grad_mixed = lax.dynamic_update_slice(grad_mixed, rows, (owner_row(s), 0))

    full_grad = in_order(grad_blocks)
    full_act = in_order(acts)
    full_two = in_order(twos)
    full_hidden_grad = in_order(hidden_grads)
    contract_weight_grad = dot("tf,td->fd", full_act, full_grad).astype(bf16)
    contract_weight_grad = lax.psum(contract_weight_grad, "dp")
    expand_weight_grad = dot("td,tf->df", full_two, full_hidden_grad).astype(bf16)
    expand_weight_grad = lax.psum(after(expand_weight_grad, contract_weight_grad), "dp")

    grad_projected = attend_backward(
        lengths, queries, keys, values, grad_mixed, mixed, lse, tables
    )
    merge_weight_grad = dot("tf,td->fd", mixed, full_grad).astype(bf16)
    full_one = in_order(ones)
    attend_weight_grad = dot("td,cte->cde", full_one, grad_projected).astype(bf16)
    attend_weight_grad, merge_weight_grad = lax.psum(
        (after(attend_weight_grad, expand_weight_grad), after(merge_weight_grad, expand_weight_grad)),
        "dp",
    )

    carried = None
    vectors = jnp.zeros((4, width), f32)
    for s in order:
        grads_rows = lax.dynamic_slice(
            grad_projected, (0, owner_row(s), 0), (3, rows_here, local_width)
        )
        grad_one = dot("cte,cde->td", grads_rows, attend_weight)
        grad_two = dot("tf,df->td", hidden_grads[s], expand_weight)
        hat, inverse = standardize(token_blocks[s].astype(f32))
        vectors = vectors + jnp.stack(
            [
                jnp.sum(grad_one * hat, axis=0),
                jnp.sum(grad_one, axis=0),
                jnp.sum(grad_two * hat, axis=0),
                jnp.sum(grad_two, axis=0),
            ]
        )
        part = grad_one * first_gain + grad_two * second_gain
        if carried is not None:
            part = part + carried.astype(f32)
        if s:
            carried = lax.ppermute(part.astype(bf16), "mp", hops)
    input_term = (
        part
        - jnp.mean(part, axis=-1, keepdims=True)
        - hat * jnp.mean(part * hat, axis=-1, keepdims=True)
    ) * inverse
    tokens_grad = (grad_out.astype(f32) + input_term).astype(bf16)

    own_biases = jnp.concatenate(
        [
            jnp.sum(grad_projected, axis=1, dtype=f32).reshape(-1),
            jnp.sum(full_hidden_grad, axis=0, dtype=f32),
        ]
    )
    slots = jnp.where(jnp.arange(ring)[:, None] == place, own_biases[None, :], 0.0)
    summed = lax.psum(
        jnp.concatenate(
            [vectors.reshape(-1), jnp.sum(grad_out, axis=0, dtype=f32), slots.reshape(-1)]
        ),
        ("dp", "mp"),
    )
    heads_at = 5 * width
    first_gain_grad, first_shift_grad, second_gain_grad, second_shift_grad, bias_total = (
        summed[:heads_at].reshape(5, width)
    )
    biases = lax.dynamic_slice(
        summed[heads_at:].reshape(ring, -1), (place, 0), (1, own_biases.shape[0])
    )[0]
    attend_bias_grad = biases[: 3 * local_width].reshape(3, local_width)
    expand_bias_grad = biases[3 * local_width :]
    return (
        layer_output,
        tokens_grad,
        first_gain_grad,
        first_shift_grad,
        second_gain_grad,
        second_shift_grad,
        attend_weight_grad.astype(f32),
        attend_bias_grad,
        merge_weight_grad.astype(f32),
        bias_total,
        expand_weight_grad.astype(f32),
        expand_bias_grad,
        contract_weight_grad.astype(f32),
        bias_total,
    )


def solution(mesh):
    rows = P(("dp", "mp"), None)
    columns, row_split = P(None, "mp"), P("mp", None)
    return jax.shard_map(
        on_device,
        mesh=mesh,
        in_specs=(
            rows,
            P("dp"),
            rows,
            P(),
            P(),
            P(),
            P(),
            P(None, None, "mp"),
            columns,
            row_split,
            P(),
            columns,
            P("mp"),
            row_split,
            P(),
        ),
        out_specs=(
            rows,
            rows,
            P(),
            P(),
            P(),
            P(),
            P(None, None, "mp"),
            columns,
            row_split,
            P(),
            columns,
            P("mp"),
            row_split,
            P(),
        ),
        check_vma=False,
    )
```

```python
from functools import partial

import jax
import jax.numpy as jnp
from jax import lax
from jax.experimental import pallas as pl
from jax.experimental.pallas import tpu as pltpu
from jax.sharding import PartitionSpec as P

HD = 256
ROT = 64
LANES = 128

norm_eps = 1e-05
masked_score = -1e30


def standardize(inputs):
    average = jnp.mean(inputs, axis=-1, keepdims=True)
    centred = inputs - average
    variance = jnp.mean(centred * centred, axis=-1, keepdims=True)
    inverse = lax.rsqrt(variance + norm_eps)
    return (centred * inverse, inverse)


def rotary_tables(length, rotated):
    halfway = rotated // 2
    channel = jnp.arange(halfway).astype(jnp.float32)
    frequency = 1.0 / 10000.0 ** (channel * 2.0 / rotated)
    positions = jnp.arange(length).astype(jnp.float32)
    angles = positions[:, None] * frequency[None, :]
    cosine, sine = jnp.cos(angles), jnp.sin(angles)
    rest = LANES - rotated
    ones, zeros = jnp.ones((length, rest), jnp.float32), jnp.zeros((length, rest), jnp.float32)
    none = jnp.zeros_like(sine)
    return (
        jnp.concatenate([cosine, cosine, ones], axis=1),
        jnp.concatenate([-sine, none, zeros], axis=1),
        jnp.concatenate([none, sine, zeros], axis=1),
    )


def turn_block(block, cosine, minus, plus, halfway):
    lead = block[:, :LANES]
    after = pltpu.roll(lead, LANES - halfway, 1)
    before = pltpu.roll(lead, halfway, 1)
    turned = lead * cosine + after * minus + before * plus
    return jnp.concatenate([turned, block[:, LANES:]], axis=1)


def forward_kernel(
    lengths, q_in, k_in, v_in, cos_q, min_q, plu_q, cos_k, min_k, plu_k,
    q_out, k_out, v_out, mixed_out, lse_out, *, rows, head_scale,
):
    step = pl.program_id(1)
    length = lengths[0]

    @pl.when(step == 0)
    def _():
        k_out[...] = turn_block(k_in[0], cos_k[...], min_k[...], plu_k[...], ROT // 2).astype(
            jnp.bfloat16
        )
        v_out[...] = v_in[0].astype(jnp.bfloat16)

    queries = (
        turn_block(q_in[0], cos_q[...], min_q[...], plu_q[...], ROT // 2) * head_scale
    ).astype(jnp.bfloat16)
    q_out[...] = queries

    def one_block(at, carried, diagonal):
        top, total, mixed = carried
        keys = k_out[pl.ds(at * rows, rows), :]
        values = v_out[pl.ds(at * rows, rows), :]
        scores = lax.dot_general(
            queries, keys, (((1,), (1,)), ((), ())), preferred_element_type=jnp.float32
        )
        places = lax.broadcasted_iota(jnp.int32, (rows, rows), 1)
        kept = places < length - at * rows
        if diagonal:
            kept = kept & (places <= lax.broadcasted_iota(jnp.int32, (rows, rows), 0))
        scores = jnp.where(kept, scores, masked_score)
        new_top = jnp.maximum(top, jnp.max(scores, axis=1, keepdims=True))
        shrink = jnp.exp(top - new_top)
        exponent = jnp.exp(scores - new_top)
        total = total * shrink + jnp.sum(exponent, axis=1, keepdims=True)
        mixed = mixed * shrink + lax.dot_general(
            exponent.astype(jnp.bfloat16),
            values,
            (((1,), (0,)), ((), ())),
            preferred_element_type=jnp.float32,
        )
        return (new_top, total, mixed)

    start = (
        jnp.full((rows, 1), masked_score, jnp.float32),
        jnp.zeros((rows, 1), jnp.float32),
        jnp.zeros((rows, HD), jnp.float32),
    )
    carried = lax.fori_loop(0, step, lambda at, c: one_block(at, c, False), start)
    top, total, mixed = one_block(step, carried, True)
    mixed_out[...] = (mixed / total).astype(jnp.bfloat16)
    lse_out[0] = top + jnp.log(total)


def backward_kernel(
    lengths, q_in, k_in, v_in, grad_in, mixed_in, lse_in, cosine, minus, plus,
    grads_out, key_sum, value_sum, *, rows, steps, head_scale,
):
    step = pl.program_id(1)
    length = lengths[0]

    @pl.when(step == 0)
    def _():
        key_sum[...] = jnp.zeros_like(key_sum)
        value_sum[...] = jnp.zeros_like(value_sum)

    queries = q_in[...]
    grads = grad_in[...]
    centre = jnp.sum(
        grads.astype(jnp.float32) * mixed_in[...].astype(jnp.float32), axis=1, keepdims=True
    )
    log_sum = lse_in[0]

    def one_block(at, grad_q, diagonal):
        span = pl.ds(at * rows, rows)
        keys = k_in[span, :]
        values = v_in[span, :]
        scores = lax.dot_general(
            queries, keys, (((1,), (1,)), ((), ())), preferred_element_type=jnp.float32
        )
        places = lax.broadcasted_iota(jnp.int32, (rows, rows), 1)
        kept = places < length - at * rows
        if diagonal:
            kept = kept & (places <= lax.broadcasted_iota(jnp.int32, (rows, rows), 0))
        weights = jnp.exp(jnp.where(kept, scores, masked_score) - log_sum)
        grad_w = lax.dot_general(
            grads, values, (((1,), (1,)), ((), ())), preferred_element_type=jnp.float32
        )
        grad_s = (weights * (grad_w - centre)).astype(jnp.bfloat16)
        key_sum[span, :] += lax.dot_general(
            grad_s, queries, (((0,), (0,)), ((), ())), preferred_element_type=jnp.float32
        )
        value_sum[span, :] += lax.dot_general(
            weights.astype(jnp.bfloat16),
            grads,
            (((0,), (0,)), ((), ())),
            preferred_element_type=jnp.float32,
        )
        return grad_q + lax.dot_general(
            grad_s, keys, (((1,), (0,)), ((), ())), preferred_element_type=jnp.float32
        )

    grad_q = lax.fori_loop(
        0, step, lambda at, c: one_block(at, c, False), jnp.zeros((rows, HD), jnp.float32)
    )
    grad_q = one_block(step, grad_q, True)
    here = pl.ds(step * rows, rows)
    grads_out[0, here, :] = (
        turn_block(grad_q, cosine[here, :], -minus[here, :], -plus[here, :], ROT // 2) * head_scale
    ).astype(jnp.bfloat16)

    @pl.when(step == steps - 1)
    def _():
        grads_out[1] = turn_block(
            key_sum[...], cosine[...], -minus[...], -plus[...], ROT // 2
        ).astype(jnp.bfloat16)
        grads_out[2] = value_sum[...].astype(jnp.bfloat16)


def attend_forward(projected, lengths, tables):
    _, span, width = projected.shape
    heads = width // HD
    rows = min(512, span)
    steps = span // rows
    low = jax.ShapeDtypeStruct((span, width), jnp.bfloat16)
    row_table = pl.BlockSpec((rows, LANES), lambda h, i, n: (i, 0))
    all_table = pl.BlockSpec((span, LANES), lambda h, i, n: (0, 0))
    row_block = pl.BlockSpec((rows, HD), lambda h, i, n: (i, h))
    all_block = pl.BlockSpec((span, HD), lambda h, i, n: (0, h))
    return pl.pallas_call(
        partial(forward_kernel, rows=rows, head_scale=HD ** (-0.5)),
        grid_spec=pltpu.PrefetchScalarGridSpec(
            num_scalar_prefetch=1,
            grid=(heads, steps),
            in_specs=[
                pl.BlockSpec((1, rows, HD), lambda h, i, n: (0, i, h)),
                pl.BlockSpec((1, span, HD), lambda h, i, n: (1, 0, h)),
                pl.BlockSpec((1, span, HD), lambda h, i, n: (2, 0, h)),
                row_table, row_table, row_table, all_table, all_table, all_table,
            ],
            out_specs=[
                row_block, all_block, all_block, row_block,
                pl.BlockSpec((1, rows, 1), lambda h, i, n: (h, i, 0)),
            ],
        ),
        out_shape=[low, low, low, low, jax.ShapeDtypeStruct((heads, span, 1), jnp.float32)],
        compiler_params=pltpu.CompilerParams(vmem_limit_bytes=48 * 1024 * 1024),
        name="attend_forward",
    )(lengths, projected, projected, projected, *tables, *tables)


def attend_backward(lengths, queries, keys, values, grad_mixed, mixed, lse, tables):
    span, width = queries.shape
    heads = width // HD
    rows = min(512, span)
    steps = span // rows
    all_table = pl.BlockSpec((span, LANES), lambda h, i, n: (0, 0))
    row_block = pl.BlockSpec((rows, HD), lambda h, i, n: (i, h))
    all_block = pl.BlockSpec((span, HD), lambda h, i, n: (0, h))
    return pl.pallas_call(
        partial(backward_kernel, rows=rows, steps=steps, head_scale=HD ** (-0.5)),
        grid_spec=pltpu.PrefetchScalarGridSpec(
            num_scalar_prefetch=1,
            grid=(heads, steps),
            in_specs=[
                row_block, all_block, all_block, row_block, row_block,
                pl.BlockSpec((1, rows, 1), lambda h, i, n: (h, i, 0)),
                all_table, all_table, all_table,
            ],
            out_specs=pl.BlockSpec((3, span, HD), lambda h, i, n: (0, 0, h)),
            scratch_shapes=[pltpu.VMEM((span, HD), jnp.float32)] * 2,
        ),
        out_shape=jax.ShapeDtypeStruct((3, span, width), jnp.bfloat16),
        compiler_params=pltpu.CompilerParams(vmem_limit_bytes=48 * 1024 * 1024),
        name="attend_backward",
    )(lengths, queries, keys, values, grad_mixed, mixed, lse, *tables)


def after(value, *others):
    return lax.optimization_barrier((value, *others))[0]


def xor_sum(vector, axis):
    size = lax.axis_size(axis)
    bit = 1
    while bit < size:
        vector = vector + lax.ppermute(vector, axis, [(i, i ^ bit) for i in range(size)])
        bit *= 2
    return vector


def cube_sum(array):
    size = lax.axis_size("dp")
    index = lax.axis_index("dp")
    bits = [1 << k for k in range(size.bit_length() - 1)]

    def exchange(value, bit):
        return lax.ppermute(value, "dp", [(i, i ^ bit) for i in range(size)])

    def halve(value, bit):
        half = value.shape[0] // 2
        side = (index // bit) % 2
        kept = lax.dynamic_slice_in_dim(value, side * half, half, 0)
        sent = lax.dynamic_slice_in_dim(value, (1 - side) * half, half, 0)
        got = exchange(sent, bit)
        return (kept.astype(jnp.float32) + got.astype(jnp.float32)).astype(value.dtype)

    def restore(value, bit):
        got = exchange(value, bit)
        upper = (index // bit) % 2 == 1
        return (jnp.where(upper, got, value), jnp.where(upper, value, got))

    array = halve(array, bits[0])
    middle = array.shape[0] // 2
    parts = []
    for part, order in ((array[:middle], bits[1:]), (array[middle:], bits[2:] + bits[1:2])):
        for bit in order:
            part = halve(part, bit)
        for bit in reversed(order):
            part = jnp.concatenate(restore(part, bit), axis=0)
        parts.append(part)
    whole = restore(jnp.concatenate(parts, axis=0), bits[0])
    return jnp.concatenate([half.astype(jnp.float32) for half in whole], axis=0)


def on_device(
    tokens,
    lengths,
    cotangent,
    first_gain,
    first_shift,
    second_gain,
    second_shift,
    attend_weight,
    attend_bias,
    merge_weight,
    merge_bias,
    expand_weight,
    expand_bias,
    contract_weight,
    contract_bias,
):
    ring = lax.axis_size("mp")
    place = lax.axis_index("mp")
    rows_here, width = tokens.shape
    group_rows = rows_here * ring
    local_width = attend_weight.shape[2]
    f32, bf16 = jnp.float32, jnp.bfloat16
    dot = partial(jnp.einsum, preferred_element_type=f32)
    up = [(i, (i + 1) % ring) for i in range(ring)]
    down = [(i, (i - 1) % ring) for i in range(ring)]
    up_hops = ring // 2
    down_hops = ring - 1 - up_hops

    def owner_row(s):
        return ((place - s) % ring) * rows_here

    def gather_blocks(block):
        blocks = {0: block}
        for s in range(1, up_hops + 1):
            blocks[s] = lax.ppermute(blocks[s - 1], "mp", up)
        for s in range(1, down_hops + 1):
            blocks[ring - s] = lax.ppermute(blocks[(ring - s + 1) % ring], "mp", down)
        return blocks

    arrival = [0]
    for s in range(1, up_hops + 1):
        arrival += [s] + ([ring - s] if s <= down_hops else [])

    def scatter_blocks(part_of, first_after=()):
        total = part_of(0)
        for hops, count, sign in ((up, up_hops, -1), (down, down_hops, 1)):
            carried = None
            for k in range(count, 0, -1):
                part = part_of(sign * k % ring)
                if carried is not None:
                    part = part + carried.astype(f32)
                part = part.astype(bf16)
                if carried is None and first_after:
                    part = after(part, *first_after)
                carried = lax.ppermute(part, "mp", hops)
            if carried is not None:
                total = total + carried.astype(f32)
        return total

    def in_order(blocks):
        whole = jnp.zeros((group_rows, blocks[0].shape[1]), blocks[0].dtype)
        for s in arrival:
            whole = lax.dynamic_update_slice(whole, blocks[s], (owner_row(s), 0))
        return whole

    tables = rotary_tables(group_rows, ROT)

    token_blocks = gather_blocks(tokens)
    row_ids = place * rows_here + jnp.arange(rows_here)
    valid_rows = row_ids < lengths[0]
    grad_out = jnp.where(valid_rows[:, None], cotangent, jnp.zeros_like(cotangent))
    grad_blocks = gather_blocks(after(grad_out, token_blocks[1], token_blocks[ring - 1]))

    projected = jnp.zeros((3, group_rows, local_width), f32)
    ones, twos, acts, slopes = {}, {}, {}, {}
    for s in arrival:
        hat, _ = standardize(token_blocks[s].astype(f32))
        ones[s] = (hat * first_gain + first_shift).astype(bf16)
        twos[s] = (hat * second_gain + second_shift).astype(bf16)
        part = dot("td,cde->cte", ones[s], attend_weight) + attend_bias[:, None, :]
        projected = lax.dynamic_update_slice(projected, part, (0, owner_row(s), 0))
        hidden = dot("td,df->tf", twos[s], expand_weight) + expand_bias
        spread = 0.5 * (1.0 + lax.erf(hidden * (0.5**0.5)))
        bell = jnp.exp(-0.5 * hidden * hidden) * 0.3989422804014327
        acts[s] = (hidden * spread).astype(bf16)
        slopes[s] = (spread + hidden * bell).astype(bf16)

    queries, keys, values, mixed, lse = attend_forward(projected, lengths, tables)

    hidden_grads = {}
    grad_mixed = jnp.zeros((group_rows, local_width), bf16)
    for s in arrival:
        grad_act = dot("td,fd->tf", grad_blocks[s], contract_weight)
        hidden_grads[s] = (grad_act * slopes[s].astype(f32)).astype(bf16)
        rows = dot("td,fd->tf", grad_blocks[s], merge_weight).astype(bf16)
        grad_mixed = lax.dynamic_update_slice(grad_mixed, rows, (owner_row(s), 0))

    full_grad = in_order(grad_blocks)
    full_hidden_grad = in_order(hidden_grads)
    contract_weight_grad = dot("tf,td->fd", in_order(acts), full_grad).astype(bf16)
    expand_weight_grad = dot("td,tf->df", in_order(twos), full_hidden_grad).astype(bf16)
    merge_weight_grad = dot("tf,td->fd", mixed, full_grad).astype(bf16)
    grad_mixed = after(grad_mixed, contract_weight_grad, expand_weight_grad)
    contract_weight_grad = cube_sum(contract_weight_grad)
    expand_weight_grad = cube_sum(expand_weight_grad)
    merge_weight_grad = cube_sum(merge_weight_grad)

    def branch_part(s):
        mixed_rows = lax.dynamic_slice(mixed, (owner_row(s), 0), (rows_here, local_width))
        return dot("tf,fd->td", mixed_rows, merge_weight) + dot(
            "tf,fd->td", acts[s], contract_weight
        )

    branches = scatter_blocks(branch_part, (grad_blocks[up_hops],))
    layer_output = (tokens.astype(f32) + branches + merge_bias + contract_bias).astype(bf16)

    grad_projected = attend_backward(
        lengths, queries, keys, values, grad_mixed, mixed, lse, tables
    )
    attend_weight_grad = dot("td,cte->cde", in_order(ones), grad_projected).astype(bf16)
    attend_weight_grad = cube_sum(attend_weight_grad.reshape(3 * width, local_width))

    vectors = []

    def normed_part(s):
        grads_rows = lax.dynamic_slice(
            grad_projected, (0, owner_row(s), 0), (3, rows_here, local_width)
        )
        grad_one = dot("cte,cde->td", grads_rows, attend_weight)
        grad_two = dot("tf,df->td", hidden_grads[s], expand_weight)
        hat, _ = standardize(token_blocks[s].astype(f32))
        vectors.append(
            jnp.stack(
                [
                    jnp.sum(grad_one * hat, axis=0),
                    jnp.sum(grad_one, axis=0),
                    jnp.sum(grad_two * hat, axis=0),
                    jnp.sum(grad_two, axis=0),
                ]
            )
        )
        return grad_one * first_gain + grad_two * second_gain

    weighted = scatter_blocks(normed_part)
    hat, inverse = standardize(tokens.astype(f32))
    input_term = (
        weighted
        - jnp.mean(weighted, axis=-1, keepdims=True)
        - hat * jnp.mean(weighted * hat, axis=-1, keepdims=True)
    ) * inverse
    tokens_grad = (grad_out.astype(f32) + input_term).astype(bf16)

    summed = jnp.concatenate(
        [
            sum(vectors).reshape(-1),
            jnp.sum(grad_out, axis=0, dtype=f32),
            jnp.sum(grad_projected, axis=1, dtype=f32).reshape(-1),
            jnp.sum(full_hidden_grad, axis=0, dtype=f32),
        ]
    )
    summed = xor_sum(summed, "dp")
    heads_at = 5 * width
    first_gain_grad, first_shift_grad, second_gain_grad, second_shift_grad, bias_total = xor_sum(
        summed[:heads_at], "mp"
    ).reshape(5, width)
    biases = summed[heads_at:]
    attend_bias_grad = biases[: 3 * local_width].reshape(3, local_width)
    expand_bias_grad = biases[3 * local_width :]
    attend_weight_grad = attend_weight_grad.reshape(attend_weight.shape)
    return (
        layer_output,
        tokens_grad,
        first_gain_grad,
        first_shift_grad,
        second_gain_grad,
        second_shift_grad,
        attend_weight_grad,
        attend_bias_grad,
        merge_weight_grad,
        bias_total,
        expand_weight_grad,
        expand_bias_grad,
        contract_weight_grad,
        bias_total,
    )


def solution(mesh):
    rows = P(("dp", "mp"), None)
    columns, row_split = P(None, "mp"), P("mp", None)
    return jax.shard_map(
        on_device,
        mesh=mesh,
        in_specs=(
            rows,
            P("dp"),
            rows,
            P(),
            P(),
            P(),
            P(),
            P(None, None, "mp"),
            columns,
            row_split,
            P(),
            columns,
            P("mp"),
            row_split,
            P(),
        ),
        out_specs=(
            rows,
            rows,
            P(),
            P(),
            P(),
            P(),
            P(None, None, "mp"),
            columns,
            row_split,
            P(),
            columns,
            P("mp"),
            row_split,
            P(),
        ),
        check_vma=False,
    )
```

```python
from functools import partial

import jax
import jax.numpy as jnp
from jax import lax
from jax.experimental import pallas as pl
from jax.experimental.pallas import tpu as pltpu
from jax.sharding import PartitionSpec as P

HD = 256
ROT = 64
LANES = 128

norm_eps = 1e-05
masked_score = -1e30


def standardize(inputs):
    average = jnp.mean(inputs, axis=-1, keepdims=True)
    centred = inputs - average
    variance = jnp.mean(centred * centred, axis=-1, keepdims=True)
    inverse = lax.rsqrt(variance + norm_eps)
    return (centred * inverse, inverse)


def rotary_tables(length, rotated):
    halfway = rotated // 2
    channel = jnp.arange(halfway).astype(jnp.float32)
    frequency = 1.0 / 10000.0 ** (channel * 2.0 / rotated)
    positions = jnp.arange(length).astype(jnp.float32)
    angles = positions[:, None] * frequency[None, :]
    cosine, sine = jnp.cos(angles), jnp.sin(angles)
    rest = LANES - rotated
    ones, zeros = jnp.ones((length, rest), jnp.float32), jnp.zeros((length, rest), jnp.float32)
    none = jnp.zeros_like(sine)
    return (
        jnp.concatenate([cosine, cosine, ones], axis=1),
        jnp.concatenate([-sine, none, zeros], axis=1),
        jnp.concatenate([none, sine, zeros], axis=1),
    )


def turn_block(block, cosine, minus, plus, halfway):
    lead = block[:, :LANES]
    after = pltpu.roll(lead, LANES - halfway, 1)
    before = pltpu.roll(lead, halfway, 1)
    turned = lead * cosine + after * minus + before * plus
    return jnp.concatenate([turned, block[:, LANES:]], axis=1)


def forward_kernel(
    lengths, q_in, k_in, v_in, cos_q, min_q, plu_q, cos_k, min_k, plu_k,
    q_out, k_out, v_out, mixed_out, lse_out, *, rows, head_scale,
):
    step = pl.program_id(1)
    length = lengths[0]

    @pl.when(step == 0)
    def _():
        k_out[...] = turn_block(k_in[0], cos_k[...], min_k[...], plu_k[...], ROT // 2).astype(
            jnp.bfloat16
        )
        v_out[...] = v_in[0].astype(jnp.bfloat16)

    queries = (
        turn_block(q_in[0], cos_q[...], min_q[...], plu_q[...], ROT // 2) * head_scale
    ).astype(jnp.bfloat16)
    q_out[...] = queries

    def one_block(at, carried, diagonal):
        top, total, mixed = carried
        keys = k_out[pl.ds(at * rows, rows), :]
        values = v_out[pl.ds(at * rows, rows), :]
        scores = lax.dot_general(
            queries, keys, (((1,), (1,)), ((), ())), preferred_element_type=jnp.float32
        )
        places = lax.broadcasted_iota(jnp.int32, (rows, rows), 1)
        kept = places < length - at * rows
        if diagonal:
            kept = kept & (places <= lax.broadcasted_iota(jnp.int32, (rows, rows), 0))
        scores = jnp.where(kept, scores, masked_score)
        new_top = jnp.maximum(top, jnp.max(scores, axis=1, keepdims=True))
        shrink = jnp.exp(top - new_top)
        exponent = jnp.exp(scores - new_top)
        total = total * shrink + jnp.sum(exponent, axis=1, keepdims=True)
        mixed = mixed * shrink + lax.dot_general(
            exponent.astype(jnp.bfloat16),
            values,
            (((1,), (0,)), ((), ())),
            preferred_element_type=jnp.float32,
        )
        return (new_top, total, mixed)

    start = (
        jnp.full((rows, 1), masked_score, jnp.float32),
        jnp.zeros((rows, 1), jnp.float32),
        jnp.zeros((rows, HD), jnp.float32),
    )
    carried = lax.fori_loop(0, step, lambda at, c: one_block(at, c, False), start)
    top, total, mixed = one_block(step, carried, True)
    mixed_out[...] = (mixed / total).astype(jnp.bfloat16)
    lse_out[0] = top + jnp.log(total)


def backward_kernel(
    lengths, q_in, k_in, v_in, grad_in, mixed_in, lse_in, cosine, minus, plus,
    grads_out, key_sum, value_sum, *, rows, steps, head_scale,
):
    step = pl.program_id(1)
    length = lengths[0]

    @pl.when(step == 0)
    def _():
        key_sum[...] = jnp.zeros_like(key_sum)
        value_sum[...] = jnp.zeros_like(value_sum)

    queries = q_in[...]
    grads = grad_in[...]
    centre = jnp.sum(
        grads.astype(jnp.float32) * mixed_in[...].astype(jnp.float32), axis=1, keepdims=True
    )
    log_sum = lse_in[0]

    def one_block(at, grad_q, diagonal):
        span = pl.ds(at * rows, rows)
        keys = k_in[span, :]
        values = v_in[span, :]
        scores = lax.dot_general(
            queries, keys, (((1,), (1,)), ((), ())), preferred_element_type=jnp.float32
        )
        places = lax.broadcasted_iota(jnp.int32, (rows, rows), 1)
        kept = places < length - at * rows
        if diagonal:
            kept = kept & (places <= lax.broadcasted_iota(jnp.int32, (rows, rows), 0))
        weights = jnp.exp(jnp.where(kept, scores, masked_score) - log_sum)
        grad_w = lax.dot_general(
            grads, values, (((1,), (1,)), ((), ())), preferred_element_type=jnp.float32
        )
        grad_s = (weights * (grad_w - centre)).astype(jnp.bfloat16)
        key_sum[span, :] += lax.dot_general(
            grad_s, queries, (((0,), (0,)), ((), ())), preferred_element_type=jnp.float32
        )
        value_sum[span, :] += lax.dot_general(
            weights.astype(jnp.bfloat16),
            grads,
            (((0,), (0,)), ((), ())),
            preferred_element_type=jnp.float32,
        )
        return grad_q + lax.dot_general(
            grad_s, keys, (((1,), (0,)), ((), ())), preferred_element_type=jnp.float32
        )

    grad_q = lax.fori_loop(
        0, step, lambda at, c: one_block(at, c, False), jnp.zeros((rows, HD), jnp.float32)
    )
    grad_q = one_block(step, grad_q, True)
    here = pl.ds(step * rows, rows)
    grads_out[0, here, :] = (
        turn_block(grad_q, cosine[here, :], -minus[here, :], -plus[here, :], ROT // 2) * head_scale
    ).astype(jnp.bfloat16)

    @pl.when(step == steps - 1)
    def _():
        grads_out[1] = turn_block(
            key_sum[...], cosine[...], -minus[...], -plus[...], ROT // 2
        ).astype(jnp.bfloat16)
        grads_out[2] = value_sum[...].astype(jnp.bfloat16)


def attend_forward(projected, lengths, tables):
    _, span, width = projected.shape
    heads = width // HD
    rows = min(512, span)
    steps = span // rows
    low = jax.ShapeDtypeStruct((span, width), jnp.bfloat16)
    row_table = pl.BlockSpec((rows, LANES), lambda h, i, n: (i, 0))
    all_table = pl.BlockSpec((span, LANES), lambda h, i, n: (0, 0))
    row_block = pl.BlockSpec((rows, HD), lambda h, i, n: (i, h))
    all_block = pl.BlockSpec((span, HD), lambda h, i, n: (0, h))
    return pl.pallas_call(
        partial(forward_kernel, rows=rows, head_scale=HD ** (-0.5)),
        grid_spec=pltpu.PrefetchScalarGridSpec(
            num_scalar_prefetch=1,
            grid=(heads, steps),
            in_specs=[
                pl.BlockSpec((1, rows, HD), lambda h, i, n: (0, i, h)),
                pl.BlockSpec((1, span, HD), lambda h, i, n: (1, 0, h)),
                pl.BlockSpec((1, span, HD), lambda h, i, n: (2, 0, h)),
                row_table, row_table, row_table, all_table, all_table, all_table,
            ],
            out_specs=[
                row_block, all_block, all_block, row_block,
                pl.BlockSpec((1, rows, 1), lambda h, i, n: (h, i, 0)),
            ],
        ),
        out_shape=[low, low, low, low, jax.ShapeDtypeStruct((heads, span, 1), jnp.float32)],
        compiler_params=pltpu.CompilerParams(vmem_limit_bytes=48 * 1024 * 1024),
        name="attend_forward",
    )(lengths, projected, projected, projected, *tables, *tables)


def attend_backward(lengths, queries, keys, values, grad_mixed, mixed, lse, tables):
    span, width = queries.shape
    heads = width // HD
    rows = min(512, span)
    steps = span // rows
    all_table = pl.BlockSpec((span, LANES), lambda h, i, n: (0, 0))
    row_block = pl.BlockSpec((rows, HD), lambda h, i, n: (i, h))
    all_block = pl.BlockSpec((span, HD), lambda h, i, n: (0, h))
    return pl.pallas_call(
        partial(backward_kernel, rows=rows, steps=steps, head_scale=HD ** (-0.5)),
        grid_spec=pltpu.PrefetchScalarGridSpec(
            num_scalar_prefetch=1,
            grid=(heads, steps),
            in_specs=[
                row_block, all_block, all_block, row_block, row_block,
                pl.BlockSpec((1, rows, 1), lambda h, i, n: (h, i, 0)),
                all_table, all_table, all_table,
            ],
            out_specs=pl.BlockSpec((3, span, HD), lambda h, i, n: (0, 0, h)),
            scratch_shapes=[pltpu.VMEM((span, HD), jnp.float32)] * 2,
        ),
        out_shape=jax.ShapeDtypeStruct((3, span, width), jnp.bfloat16),
        compiler_params=pltpu.CompilerParams(vmem_limit_bytes=48 * 1024 * 1024),
        name="attend_backward",
    )(lengths, queries, keys, values, grad_mixed, mixed, lse, *tables)


def after(value, *others):
    return lax.optimization_barrier((value, *others))[0]


def tie(values, others):
    return lax.optimization_barrier((*values, *others))[: len(values)]


def xor_sum(vector, axis):
    size = lax.axis_size(axis)
    bit = 1
    while bit < size:
        vector = vector + lax.ppermute(vector, axis, [(i, i ^ bit) for i in range(size)])
        bit *= 2
    return vector


def cube_sum(array):
    size = lax.axis_size("dp")
    index = lax.axis_index("dp")
    bits = [1 << k for k in range(size.bit_length() - 1)]

    def exchange(value, bit):
        return lax.ppermute(value, "dp", [(i, i ^ bit) for i in range(size)])

    def halve(value, bit):
        half = value.shape[0] // 2
        side = (index // bit) % 2
        kept = lax.dynamic_slice_in_dim(value, side * half, half, 0)
        sent = lax.dynamic_slice_in_dim(value, (1 - side) * half, half, 0)
        got = exchange(sent, bit)
        return (kept.astype(jnp.float32) + got.astype(jnp.float32)).astype(value.dtype)

    def restore(value, bit):
        got = exchange(value, bit)
        upper = (index // bit) % 2 == 1
        return (jnp.where(upper, got, value), jnp.where(upper, value, got))

    array = halve(array, bits[0])
    yield (array,)
    middle = array.shape[0] // 2
    parts = [array[:middle], array[middle:]]
    orders = [bits[1:], bits[2:] + bits[1:2]]
    levels = range(len(bits) - 1)
    for level in levels:
        parts = [halve(part, order[level]) for part, order in zip(parts, orders)]
        yield tuple(parts)
    for level in reversed(levels):
        parts = [
            jnp.concatenate(restore(part, order[level]), axis=0)
            for part, order in zip(parts, orders)
        ]
        yield tuple(parts)
    whole = restore(jnp.concatenate(parts, axis=0), bits[0])
    yield (jnp.concatenate([half.astype(jnp.float32) for half in whole], axis=0),)


class Sums:
    def __init__(self):
        self.running = {}
        self.totals = {}

    def add(self, name, array):
        self.running[name] = cube_sum(array)

    def step(self):
        moved = []
        for name, stages in list(self.running.items()):
            latest = next(stages, None)
            if latest is None:
                del self.running[name]
            else:
                self.totals[name] = latest[0]
                moved += latest
        return moved

    def finish(self):
        while self.running:
            self.step()
        return self.totals


def on_device(
    tokens,
    lengths,
    cotangent,
    first_gain,
    first_shift,
    second_gain,
    second_shift,
    attend_weight,
    attend_bias,
    merge_weight,
    merge_bias,
    expand_weight,
    expand_bias,
    contract_weight,
    contract_bias,
):
    ring = lax.axis_size("mp")
    place = lax.axis_index("mp")
    rows_here, width = tokens.shape
    group_rows = rows_here * ring
    local_width = attend_weight.shape[2]
    f32, bf16 = jnp.float32, jnp.bfloat16
    dot = partial(jnp.einsum, preferred_element_type=f32)
    up = [(i, (i + 1) % ring) for i in range(ring)]
    down = [(i, (i - 1) % ring) for i in range(ring)]
    up_hops = ring // 2
    down_hops = ring - 1 - up_hops

    def owner_row(s):
        return ((place - s) % ring) * rows_here

    def gather_blocks(block):
        blocks = {0: block}
        for s in range(1, up_hops + 1):
            blocks[s] = lax.ppermute(blocks[s - 1], "mp", up)
        for s in range(1, down_hops + 1):
            blocks[ring - s] = lax.ppermute(blocks[(ring - s + 1) % ring], "mp", down)
        return blocks

    arrival = [0]
    for s in range(1, up_hops + 1):
        arrival += [s] + ([ring - s] if s <= down_hops else [])

    scatter_order = []
    for k in range(max(up_hops, down_hops)):
        if k < up_hops:
            scatter_order.append(("up", -(up_hops - k) % ring))
        if k < down_hops:
            scatter_order.append(("down", down_hops - k))

    def scatter_blocks(part_of, first_after=()):
        carried, arrived = {}, []
        for way, s in scatter_order:
            part = part_of(s)
            if way in carried:
                part = part + carried[way].astype(f32)
            part = part.astype(bf16)
            if way not in carried and first_after:
                part = after(part, *first_after)
            carried[way] = lax.ppermute(part, "mp", up if way == "up" else down)
            arrived.append(carried[way])
        total = part_of(0)
        for rows in carried.values():
            total = total + rows.astype(f32)
        return total, arrived

    def in_order(blocks):
        whole = jnp.zeros((group_rows, blocks[0].shape[1]), blocks[0].dtype)
        for s in arrival:
            whole = lax.dynamic_update_slice(whole, blocks[s], (owner_row(s), 0))
        return whole

    tables = rotary_tables(group_rows, ROT)

    token_blocks = gather_blocks(tokens)
    row_ids = place * rows_here + jnp.arange(rows_here)
    valid_rows = row_ids < lengths[0]
    grad_out = jnp.where(valid_rows[:, None], cotangent, jnp.zeros_like(cotangent))
    grad_blocks = gather_blocks(after(grad_out, token_blocks[up_hops]))
    grad_blocks[0] = after(grad_blocks[0], grad_blocks[1], grad_blocks[ring - 1])

    projected = jnp.zeros((3, group_rows, local_width), f32)
    ones, twos, acts, slopes = {}, {}, {}, {}
    for s in arrival:
        hat, _ = standardize(token_blocks[s].astype(f32))
        ones[s] = (hat * first_gain + first_shift).astype(bf16)
        twos[s] = (hat * second_gain + second_shift).astype(bf16)
        part = dot("td,cde->cte", ones[s], attend_weight) + attend_bias[:, None, :]
        projected = lax.dynamic_update_slice(projected, part, (0, owner_row(s), 0))
        hidden = dot("td,df->tf", twos[s], expand_weight) + expand_bias
        spread = 0.5 * (1.0 + lax.erf(hidden * (0.5**0.5)))
        bell = jnp.exp(-0.5 * hidden * hidden) * 0.3989422804014327
        acts[s] = (hidden * spread).astype(bf16)
        slopes[s] = (spread + hidden * bell).astype(bf16)

    queries, keys, values, mixed, lse = attend_forward(projected, lengths, tables)

    hidden_grads = {}
    grad_mixed = jnp.zeros((group_rows, local_width), bf16)
    for s in arrival:
        grad_act = dot("td,fd->tf", grad_blocks[s], contract_weight)
        hidden_grads[s] = (grad_act * slopes[s].astype(f32)).astype(bf16)
        rows = dot("td,fd->tf", grad_blocks[s], merge_weight).astype(bf16)
        grad_mixed = lax.dynamic_update_slice(grad_mixed, rows, (owner_row(s), 0))

    def branch_part(s):
        mixed_rows = lax.dynamic_slice(mixed, (owner_row(s), 0), (rows_here, local_width))
        return dot("tf,fd->td", mixed_rows, merge_weight) + dot(
            "tf,fd->td", acts[s], contract_weight
        )

    branches, arrived = scatter_blocks(branch_part, (grad_blocks[up_hops],))
    layer_output = (tokens.astype(f32) + branches + merge_bias + contract_bias).astype(bf16)

    sums = Sums()
    full_grad = in_order(grad_blocks)
    full_hidden_grad = in_order(hidden_grads)
    contract_weight_grad = dot("tf,td->fd", in_order(acts), full_grad).astype(bf16)
    sums.add("contract", contract_weight_grad)

    (full_two,) = tie((in_order(twos),), (contract_weight_grad,))
    expand_weight_grad = dot("td,tf->df", full_two, full_hidden_grad).astype(bf16)
    moved = sums.step()
    sums.add("expand", expand_weight_grad)

    grad_mixed, mixed_here = tie((grad_mixed, mixed), (expand_weight_grad, *moved))
    merge_weight_grad = dot("tf,td->fd", mixed_here, full_grad).astype(bf16)
    grad_projected = attend_backward(
        lengths, queries, keys, values, after(grad_mixed, merge_weight_grad), mixed, lse, tables
    )
    moved = sums.step()
    sums.add("merge", merge_weight_grad)

    grad_projected, full_one = tie(
        (grad_projected, in_order(ones)), (*moved, arrived[0], arrived[1])
    )
    attend_weight_grad = dot("td,cte->cde", full_one, grad_projected).astype(bf16)
    attend_weight_grad = attend_weight_grad.reshape(3 * width, local_width)
    moved = sums.step() + [attend_weight_grad]
    sums.add("attend", attend_weight_grad)

    vectors = []

    def normed_part(s):
        grads_rows = lax.dynamic_slice(
            grad_projected, (0, owner_row(s), 0), (3, rows_here, local_width)
        )
        grads_rows, hidden_rows = tie((grads_rows, hidden_grads[s]), moved)
        grad_one = dot("cte,cde->td", grads_rows, attend_weight)
        grad_two = dot("tf,df->td", hidden_rows, expand_weight)
        hat, _ = standardize(token_blocks[s].astype(f32))
        vectors.append(
            jnp.stack(
                [
                    jnp.sum(grad_one * hat, axis=0),
                    jnp.sum(grad_one, axis=0),
                    jnp.sum(grad_two * hat, axis=0),
                    jnp.sum(grad_two, axis=0),
                ]
            )
        )
        part = grad_one * first_gain + grad_two * second_gain
        moved[:] = sums.step() + [part]
        return part

    weighted, _ = scatter_blocks(normed_part)
    hat, inverse = standardize(tokens.astype(f32))
    input_term = (
        weighted
        - jnp.mean(weighted, axis=-1, keepdims=True)
        - hat * jnp.mean(weighted * hat, axis=-1, keepdims=True)
    ) * inverse
    tokens_grad = (grad_out.astype(f32) + input_term).astype(bf16)

    summed = jnp.concatenate(
        [
            sum(vectors).reshape(-1),
            jnp.sum(grad_out, axis=0, dtype=f32),
            jnp.sum(grad_projected, axis=1, dtype=f32).reshape(-1),
            jnp.sum(full_hidden_grad, axis=0, dtype=f32),
        ]
    )
    summed = xor_sum(summed, "dp")
    heads_at = 5 * width
    first_gain_grad, first_shift_grad, second_gain_grad, second_shift_grad, bias_total = xor_sum(
        summed[:heads_at], "mp"
    ).reshape(5, width)
    biases = summed[heads_at:]
    attend_bias_grad = biases[: 3 * local_width].reshape(3, local_width)
    expand_bias_grad = biases[3 * local_width :]
    totals = sums.finish()
    return (
        layer_output,
        tokens_grad,
        first_gain_grad,
        first_shift_grad,
        second_gain_grad,
        second_shift_grad,
        totals["attend"].reshape(attend_weight.shape),
        attend_bias_grad,
        totals["merge"],
        bias_total,
        totals["expand"],
        expand_bias_grad,
        totals["contract"],
        bias_total,
    )


def solution(mesh):
    rows = P(("dp", "mp"), None)
    columns, row_split = P(None, "mp"), P("mp", None)
    return jax.shard_map(
        on_device,
        mesh=mesh,
        in_specs=(
            rows,
            P("dp"),
            rows,
            P(),
            P(),
            P(),
            P(),
            P(None, None, "mp"),
            columns,
            row_split,
            P(),
            columns,
            P("mp"),
            row_split,
            P(),
        ),
        out_specs=(
            rows,
            rows,
            P(),
            P(),
            P(),
            P(),
            P(None, None, "mp"),
            columns,
            row_split,
            P(),
            columns,
            P("mp"),
            row_split,
            P(),
        ),
        check_vma=False,
    )
```

```python
from functools import partial

import jax
import jax.numpy as jnp
from jax import lax
from jax.experimental import pallas as pl
from jax.experimental.pallas import tpu as pltpu
from jax.sharding import PartitionSpec as P

HD = 256
ROT = 64
LANES = 128

norm_eps = 1e-05
masked_score = -1e30


def standardize(inputs):
    average = jnp.mean(inputs, axis=-1, keepdims=True)
    centred = inputs - average
    variance = jnp.mean(centred * centred, axis=-1, keepdims=True)
    inverse = lax.rsqrt(variance + norm_eps)
    return (centred * inverse, inverse)


def rotary_tables(length, rotated):
    halfway = rotated // 2
    channel = jnp.arange(halfway).astype(jnp.float32)
    frequency = 1.0 / 10000.0 ** (channel * 2.0 / rotated)
    positions = jnp.arange(length).astype(jnp.float32)
    angles = positions[:, None] * frequency[None, :]
    cosine, sine = jnp.cos(angles), jnp.sin(angles)
    rest = LANES - rotated
    ones, zeros = jnp.ones((length, rest), jnp.float32), jnp.zeros((length, rest), jnp.float32)
    none = jnp.zeros_like(sine)
    return (
        jnp.concatenate([cosine, cosine, ones], axis=1),
        jnp.concatenate([-sine, none, zeros], axis=1),
        jnp.concatenate([none, sine, zeros], axis=1),
    )


def turn_block(block, cosine, minus, plus, halfway):
    lead = block[:, :LANES]
    after = pltpu.roll(lead, LANES - halfway, 1)
    before = pltpu.roll(lead, halfway, 1)
    turned = lead * cosine + after * minus + before * plus
    return jnp.concatenate([turned, block[:, LANES:]], axis=1)


def forward_kernel(
    lengths, q_in, k_in, v_in, cos_q, min_q, plu_q, cos_k, min_k, plu_k,
    q_out, k_out, v_out, mixed_out, lse_out, *, rows, head_scale,
):
    step = pl.program_id(1)
    length = lengths[0]

    @pl.when(step == 0)
    def _():
        k_out[...] = turn_block(k_in[0], cos_k[...], min_k[...], plu_k[...], ROT // 2).astype(
            jnp.bfloat16
        )
        v_out[...] = v_in[0].astype(jnp.bfloat16)

    queries = (
        turn_block(q_in[0], cos_q[...], min_q[...], plu_q[...], ROT // 2) * head_scale
    ).astype(jnp.bfloat16)
    q_out[...] = queries

    def one_block(at, carried, diagonal):
        top, total, mixed = carried
        keys = k_out[pl.ds(at * rows, rows), :]
        values = v_out[pl.ds(at * rows, rows), :]
        scores = lax.dot_general(
            queries, keys, (((1,), (1,)), ((), ())), preferred_element_type=jnp.float32
        )
        places = lax.broadcasted_iota(jnp.int32, (rows, rows), 1)
        kept = places < length - at * rows
        if diagonal:
            kept = kept & (places <= lax.broadcasted_iota(jnp.int32, (rows, rows), 0))
        scores = jnp.where(kept, scores, masked_score)
        new_top = jnp.maximum(top, jnp.max(scores, axis=1, keepdims=True))
        shrink = jnp.exp(top - new_top)
        exponent = jnp.exp(scores - new_top)
        total = total * shrink + jnp.sum(exponent, axis=1, keepdims=True)
        mixed = mixed * shrink + lax.dot_general(
            exponent.astype(jnp.bfloat16),
            values,
            (((1,), (0,)), ((), ())),
            preferred_element_type=jnp.float32,
        )
        return (new_top, total, mixed)

    start = (
        jnp.full((rows, 1), masked_score, jnp.float32),
        jnp.zeros((rows, 1), jnp.float32),
        jnp.zeros((rows, HD), jnp.float32),
    )
    carried = lax.fori_loop(0, step, lambda at, c: one_block(at, c, False), start)
    top, total, mixed = one_block(step, carried, True)
    mixed_out[...] = (mixed / total).astype(jnp.bfloat16)
    lse_out[0] = top + jnp.log(total)


def backward_kernel(
    lengths, q_in, k_in, v_in, grad_in, mixed_in, lse_in, cosine, minus, plus,
    grads_out, key_sum, value_sum, *, rows, steps, head_scale,
):
    step = pl.program_id(1)
    length = lengths[0]

    @pl.when(step == 0)
    def _():
        key_sum[...] = jnp.zeros_like(key_sum)
        value_sum[...] = jnp.zeros_like(value_sum)

    queries = q_in[...]
    grads = grad_in[...]
    centre = jnp.sum(
        grads.astype(jnp.float32) * mixed_in[...].astype(jnp.float32), axis=1, keepdims=True
    )
    log_sum = lse_in[0]

    def one_block(at, grad_q, diagonal):
        span = pl.ds(at * rows, rows)
        keys = k_in[span, :]
        values = v_in[span, :]
        scores = lax.dot_general(
            queries, keys, (((1,), (1,)), ((), ())), preferred_element_type=jnp.float32
        )
        places = lax.broadcasted_iota(jnp.int32, (rows, rows), 1)
        kept = places < length - at * rows
        if diagonal:
            kept = kept & (places <= lax.broadcasted_iota(jnp.int32, (rows, rows), 0))
        weights = jnp.exp(jnp.where(kept, scores, masked_score) - log_sum)
        grad_w = lax.dot_general(
            grads, values, (((1,), (1,)), ((), ())), preferred_element_type=jnp.float32
        )
        grad_s = (weights * (grad_w - centre)).astype(jnp.bfloat16)
        key_sum[span, :] += lax.dot_general(
            grad_s, queries, (((0,), (0,)), ((), ())), preferred_element_type=jnp.float32
        )
        value_sum[span, :] += lax.dot_general(
            weights.astype(jnp.bfloat16),
            grads,
            (((0,), (0,)), ((), ())),
            preferred_element_type=jnp.float32,
        )
        return grad_q + lax.dot_general(
            grad_s, keys, (((1,), (0,)), ((), ())), preferred_element_type=jnp.float32
        )

    grad_q = lax.fori_loop(
        0, step, lambda at, c: one_block(at, c, False), jnp.zeros((rows, HD), jnp.float32)
    )
    grad_q = one_block(step, grad_q, True)
    here = pl.ds(step * rows, rows)
    grads_out[0, here, :] = (
        turn_block(grad_q, cosine[here, :], -minus[here, :], -plus[here, :], ROT // 2) * head_scale
    ).astype(jnp.bfloat16)

    @pl.when(step == steps - 1)
    def _():
        grads_out[1] = turn_block(
            key_sum[...], cosine[...], -minus[...], -plus[...], ROT // 2
        ).astype(jnp.bfloat16)
        grads_out[2] = value_sum[...].astype(jnp.bfloat16)


def attend_forward(projected, lengths, tables):
    _, span, width = projected.shape
    heads = width // HD
    rows = min(512, span)
    steps = span // rows
    low = jax.ShapeDtypeStruct((span, width), jnp.bfloat16)
    row_table = pl.BlockSpec((rows, LANES), lambda h, i, n: (i, 0))
    all_table = pl.BlockSpec((span, LANES), lambda h, i, n: (0, 0))
    row_block = pl.BlockSpec((rows, HD), lambda h, i, n: (i, h))
    all_block = pl.BlockSpec((span, HD), lambda h, i, n: (0, h))
    return pl.pallas_call(
        partial(forward_kernel, rows=rows, head_scale=HD ** (-0.5)),
        grid_spec=pltpu.PrefetchScalarGridSpec(
            num_scalar_prefetch=1,
            grid=(heads, steps),
            in_specs=[
                pl.BlockSpec((1, rows, HD), lambda h, i, n: (0, i, h)),
                pl.BlockSpec((1, span, HD), lambda h, i, n: (1, 0, h)),
                pl.BlockSpec((1, span, HD), lambda h, i, n: (2, 0, h)),
                row_table, row_table, row_table, all_table, all_table, all_table,
            ],
            out_specs=[
                row_block, all_block, all_block, row_block,
                pl.BlockSpec((1, rows, 1), lambda h, i, n: (h, i, 0)),
            ],
        ),
        out_shape=[low, low, low, low, jax.ShapeDtypeStruct((heads, span, 1), jnp.float32)],
        compiler_params=pltpu.CompilerParams(vmem_limit_bytes=48 * 1024 * 1024),
        name="attend_forward",
    )(lengths, projected, projected, projected, *tables, *tables)


def attend_backward(lengths, queries, keys, values, grad_mixed, mixed, lse, tables):
    span, width = queries.shape
    heads = width // HD
    rows = min(512, span)
    steps = span // rows
    all_table = pl.BlockSpec((span, LANES), lambda h, i, n: (0, 0))
    row_block = pl.BlockSpec((rows, HD), lambda h, i, n: (i, h))
    all_block = pl.BlockSpec((span, HD), lambda h, i, n: (0, h))
    return pl.pallas_call(
        partial(backward_kernel, rows=rows, steps=steps, head_scale=HD ** (-0.5)),
        grid_spec=pltpu.PrefetchScalarGridSpec(
            num_scalar_prefetch=1,
            grid=(heads, steps),
            in_specs=[
                row_block, all_block, all_block, row_block, row_block,
                pl.BlockSpec((1, rows, 1), lambda h, i, n: (h, i, 0)),
                all_table, all_table, all_table,
            ],
            out_specs=pl.BlockSpec((3, span, HD), lambda h, i, n: (0, 0, h)),
            scratch_shapes=[pltpu.VMEM((span, HD), jnp.float32)] * 2,
        ),
        out_shape=jax.ShapeDtypeStruct((3, span, width), jnp.bfloat16),
        compiler_params=pltpu.CompilerParams(vmem_limit_bytes=48 * 1024 * 1024),
        name="attend_backward",
    )(lengths, queries, keys, values, grad_mixed, mixed, lse, *tables)


def after(value, *others):
    return lax.optimization_barrier((value, *others))[0]


def tie(values, others):
    return lax.optimization_barrier((*values, *others))[: len(values)]


def xor_sum(vector, axis):
    size = lax.axis_size(axis)
    bit = 1
    while bit < size:
        vector = vector + lax.ppermute(vector, axis, [(i, i ^ bit) for i in range(size)])
        bit *= 2
    return vector


def cube_sum(array, gate_of):
    size = lax.axis_size("dp")
    index = lax.axis_index("dp")
    bits = [1 << k for k in range(size.bit_length() - 1)]

    def exchange(value, bit):
        got = lax.ppermute(value, "dp", [(i, i ^ bit) for i in range(size)])
        return after(got, *gate_of())

    def halve(value, bit):
        half = value.shape[0] // 2
        side = (index // bit) % 2
        kept = lax.dynamic_slice_in_dim(value, side * half, half, 0)
        sent = lax.dynamic_slice_in_dim(value, (1 - side) * half, half, 0)
        got = exchange(sent, bit)
        return (kept.astype(jnp.float32) + got.astype(jnp.float32)).astype(value.dtype)

    def restore(value, bit):
        got = exchange(value, bit)
        upper = (index // bit) % 2 == 1
        return (jnp.where(upper, got, value), jnp.where(upper, value, got))

    array = halve(array, bits[0])
    yield (array,)
    middle = array.shape[0] // 2
    parts = [array[:middle], array[middle:]]
    orders = [bits[1:], bits[2:] + bits[1:2]]
    levels = range(len(bits) - 1)
    for level in levels:
        parts = [halve(part, order[level]) for part, order in zip(parts, orders)]
        yield tuple(parts)
    for level in reversed(levels):
        parts = [
            jnp.concatenate(restore(part, order[level]), axis=0)
            for part, order in zip(parts, orders)
        ]
        yield tuple(parts)
    whole = restore(jnp.concatenate(parts, axis=0), bits[0])
    yield (jnp.concatenate([half.astype(jnp.float32) for half in whole], axis=0),)


class Sums:
    def __init__(self):
        self.running = {}
        self.totals = {}
        self.gate = ()

    def add(self, name, array):
        self.running[name] = cube_sum(array, lambda: self.gate)

    def step(self, *names, gate=()):
        moved = []
        self.gate = gate
        for name in names:
            latest = next(self.running[name], None) if name in self.running else ()
            if latest == ():
                continue
            if latest is None:
                del self.running[name]
            else:
                self.totals[name] = latest[0]
                moved += latest
        return moved

    def finish(self):
        while self.running:
            self.step(*self.running)
        return self.totals


def on_device(
    tokens,
    lengths,
    cotangent,
    first_gain,
    first_shift,
    second_gain,
    second_shift,
    attend_weight,
    attend_bias,
    merge_weight,
    merge_bias,
    expand_weight,
    expand_bias,
    contract_weight,
    contract_bias,
):
    ring = lax.axis_size("mp")
    place = lax.axis_index("mp")
    rows_here, width = tokens.shape
    group_rows = rows_here * ring
    local_width = attend_weight.shape[2]
    f32, bf16 = jnp.float32, jnp.bfloat16
    dot = partial(jnp.einsum, preferred_element_type=f32)
    up = [(i, (i + 1) % ring) for i in range(ring)]
    down = [(i, (i - 1) % ring) for i in range(ring)]
    up_hops = ring // 2
    down_hops = ring - 1 - up_hops

    def owner_row(s):
        return ((place - s) % ring) * rows_here

    def gather_blocks(block):
        blocks = {0: block}
        for s in range(1, up_hops + 1):
            blocks[s] = lax.ppermute(blocks[s - 1], "mp", up)
        for s in range(1, down_hops + 1):
            blocks[ring - s] = lax.ppermute(blocks[(ring - s + 1) % ring], "mp", down)
        return blocks

    arrival = [0]
    for s in range(1, up_hops + 1):
        arrival += [s] + ([ring - s] if s <= down_hops else [])

    scatter_order = []
    for k in range(max(up_hops, down_hops)):
        if k < up_hops:
            scatter_order.append(("up", -(up_hops - k) % ring))
        if k < down_hops:
            scatter_order.append(("down", down_hops - k))

    def scatter_blocks(part_of, first_after=()):
        carried, arrived = {}, []
        for way, s in scatter_order:
            part = part_of(s)
            if way in carried:
                part = part + carried[way].astype(f32)
            part = part.astype(bf16)
            if way not in carried and first_after:
                part = after(part, *first_after)
            carried[way] = lax.ppermute(part, "mp", up if way == "up" else down)
            arrived.append(carried[way])
        total = part_of(0)
        for rows in carried.values():
            total = total + rows.astype(f32)
        return total, arrived

    def in_order(blocks):
        whole = jnp.zeros((group_rows, blocks[0].shape[1]), blocks[0].dtype)
        for s in arrival:
            whole = lax.dynamic_update_slice(whole, blocks[s], (owner_row(s), 0))
        return whole

    tables = rotary_tables(group_rows, ROT)

    token_blocks = gather_blocks(tokens)
    row_ids = place * rows_here + jnp.arange(rows_here)
    valid_rows = row_ids < lengths[0]
    grad_out = jnp.where(valid_rows[:, None], cotangent, jnp.zeros_like(cotangent))
    grad_blocks = gather_blocks(after(grad_out, token_blocks[up_hops]))
    token_blocks[ring - 1] = after(token_blocks[ring - 1], token_blocks[up_hops])

    projected = jnp.zeros((3, group_rows, local_width), f32)
    ones, twos, acts, slopes = {}, {}, {}, {}
    for s in arrival:
        hat, _ = standardize(token_blocks[s].astype(f32))
        ones[s] = (hat * first_gain + first_shift).astype(bf16)
        twos[s] = (hat * second_gain + second_shift).astype(bf16)
        part = dot("td,cde->cte", ones[s], attend_weight) + attend_bias[:, None, :]
        projected = lax.dynamic_update_slice(projected, part, (0, owner_row(s), 0))
        hidden = dot("td,df->tf", twos[s], expand_weight) + expand_bias
        spread = 0.5 * (1.0 + lax.erf(hidden * (0.5**0.5)))
        bell = jnp.exp(-0.5 * hidden * hidden) * 0.3989422804014327
        acts[s] = (hidden * spread).astype(bf16)
        slopes[s] = (spread + hidden * bell).astype(bf16)

    queries, keys, values, mixed, lse = attend_forward(projected, lengths, tables)

    grad_blocks[0] = after(grad_blocks[0], mixed)
    hidden_grads = {}
    grad_mixed = jnp.zeros((group_rows, local_width), bf16)
    for s in arrival:
        grad_act = dot("td,fd->tf", grad_blocks[s], contract_weight)
        hidden_grads[s] = (grad_act * slopes[s].astype(f32)).astype(bf16)
        rows = dot("td,fd->tf", grad_blocks[s], merge_weight).astype(bf16)
        grad_mixed = lax.dynamic_update_slice(grad_mixed, rows, (owner_row(s), 0))

    def branch_part(s):
        mixed_rows = lax.dynamic_slice(mixed, (owner_row(s), 0), (rows_here, local_width))
        return dot("tf,fd->td", mixed_rows, merge_weight) + dot(
            "tf,fd->td", acts[s], contract_weight
        )

    branches, arrived = scatter_blocks(branch_part, (grad_blocks[up_hops],))
    layer_output = (tokens.astype(f32) + branches + merge_bias + contract_bias).astype(bf16)

    sums = Sums()
    full_grad = in_order(grad_blocks)
    full_hidden_grad = in_order(hidden_grads)
    contract_weight_grad = dot("tf,td->fd", in_order(acts), full_grad).astype(bf16)
    sums.add("contract", contract_weight_grad)

    (full_two,) = tie((in_order(twos),), (contract_weight_grad,))
    expand_weight_grad = dot("td,tf->df", full_two, full_hidden_grad).astype(bf16)
    moved = sums.step("contract", gate=(expand_weight_grad,))
    sums.add("expand", expand_weight_grad)

    (mixed_here,) = tie((mixed,), (expand_weight_grad, *moved))
    merge_weight_grad = dot("tf,td->fd", mixed_here, full_grad).astype(bf16)
    moved = sums.step("expand", gate=(merge_weight_grad,))
    sums.add("merge", merge_weight_grad)

    grad_projected = attend_backward(
        lengths,
        queries,
        keys,
        values,
        after(grad_mixed, merge_weight_grad, *moved),
        mixed,
        lse,
        tables,
    )
    moved = sums.step("contract", "merge", gate=(grad_projected,)) + arrived[:2]
    later_steps = [
        ("expand",),
        ("contract", "expand", "merge"),
        ("attend", "contract", "expand"),
        ("contract", "merge"),
        ("expand", "contract", "attend", "merge"),
    ]

    def next_step(made):
        return sums.step(*later_steps.pop(0), gate=(made,)) if later_steps else []

    def attend_segment():
        grads_here, full_one = tie((grad_projected, in_order(ones)), moved)
        made = dot("td,cte->cde", full_one, grads_here).astype(bf16)
        made = made.reshape(3 * width, local_width)
        moved[:] = next_step(made) + [made]
        sums.add("attend", made)

    vectors = []

    def normed_part(s):
        grads_rows = lax.dynamic_slice(
            grad_projected, (0, owner_row(s), 0), (3, rows_here, local_width)
        )
        grads_rows, hidden_rows = tie((grads_rows, hidden_grads[s]), moved)
        grad_one = dot("cte,cde->td", grads_rows, attend_weight)
        grad_two = dot("tf,df->td", hidden_rows, expand_weight)
        hat, _ = standardize(token_blocks[s].astype(f32))
        vectors.append(
            jnp.stack(
                [
                    jnp.sum(grad_one * hat, axis=0),
                    jnp.sum(grad_one, axis=0),
                    jnp.sum(grad_two * hat, axis=0),
                    jnp.sum(grad_two, axis=0),
                ]
            )
        )
        part = grad_one * first_gain + grad_two * second_gain
        moved[:] = next_step(part) + [part]
        if len(vectors) == 1:
            attend_segment()
        return part

    weighted, _ = scatter_blocks(normed_part)
    hat, inverse = standardize(tokens.astype(f32))
    input_term = (
        weighted
        - jnp.mean(weighted, axis=-1, keepdims=True)
        - hat * jnp.mean(weighted * hat, axis=-1, keepdims=True)
    ) * inverse
    tokens_grad = (grad_out.astype(f32) + input_term).astype(bf16)

    summed = jnp.concatenate(
        [
            sum(vectors).reshape(-1),
            jnp.sum(grad_out, axis=0, dtype=f32),
            jnp.sum(grad_projected, axis=1, dtype=f32).reshape(-1),
            jnp.sum(full_hidden_grad, axis=0, dtype=f32),
        ]
    )
    summed = xor_sum(summed, "dp")
    heads_at = 5 * width
    first_gain_grad, first_shift_grad, second_gain_grad, second_shift_grad, bias_total = xor_sum(
        summed[:heads_at], "mp"
    ).reshape(5, width)
    biases = summed[heads_at:]
    attend_bias_grad = biases[: 3 * local_width].reshape(3, local_width)
    expand_bias_grad = biases[3 * local_width :]
    totals = sums.finish()
    return (
        layer_output,
        tokens_grad,
        first_gain_grad,
        first_shift_grad,
        second_gain_grad,
        second_shift_grad,
        totals["attend"].reshape(attend_weight.shape),
        attend_bias_grad,
        totals["merge"],
        bias_total,
        totals["expand"],
        expand_bias_grad,
        totals["contract"],
        bias_total,
    )


def solution(mesh):
    rows = P(("dp", "mp"), None)
    columns, row_split = P(None, "mp"), P("mp", None)
    return jax.shard_map(
        on_device,
        mesh=mesh,
        in_specs=(
            rows,
            P("dp"),
            rows,
            P(),
            P(),
            P(),
            P(),
            P(None, None, "mp"),
            columns,
            row_split,
            P(),
            columns,
            P("mp"),
            row_split,
            P(),
        ),
        out_specs=(
            rows,
            rows,
            P(),
            P(),
            P(),
            P(),
            P(None, None, "mp"),
            columns,
            row_split,
            P(),
            columns,
            P("mp"),
            row_split,
            P(),
        ),
        check_vma=False,
    )
```

```python
import math
from functools import partial

import jax
import jax.numpy as jnp
from jax import lax
from jax.experimental import pallas as pl
from jax.experimental.pallas import tpu as pltpu
from jax.sharding import PartitionSpec as P

HD = 256
ROT = 64
LANES = 128

norm_eps = 1e-05
masked_score = -1e30


def standardize(inputs):
    average = jnp.mean(inputs, axis=-1, keepdims=True)
    centred = inputs - average
    variance = jnp.mean(centred * centred, axis=-1, keepdims=True)
    inverse = lax.rsqrt(variance + norm_eps)
    return (centred * inverse, inverse)


def rotary_tables(length, rotated):
    halfway = rotated // 2
    channel = jnp.arange(halfway).astype(jnp.float32)
    frequency = 1.0 / 10000.0 ** (channel * 2.0 / rotated)
    positions = jnp.arange(length).astype(jnp.float32)
    angles = positions[:, None] * frequency[None, :]
    cosine, sine = jnp.cos(angles), jnp.sin(angles)
    rest = LANES - rotated
    ones, zeros = jnp.ones((length, rest), jnp.float32), jnp.zeros((length, rest), jnp.float32)
    none = jnp.zeros_like(sine)
    return (
        jnp.concatenate([cosine, cosine, ones], axis=1),
        jnp.concatenate([-sine, none, zeros], axis=1),
        jnp.concatenate([none, sine, zeros], axis=1),
    )


def turn_block(block, cosine, minus, plus, halfway):
    lead = block[:, :LANES]
    after = pltpu.roll(lead, LANES - halfway, 1)
    before = pltpu.roll(lead, halfway, 1)
    turned = lead * cosine + after * minus + before * plus
    return jnp.concatenate([turned, block[:, LANES:]], axis=1)


def forward_kernel(
    lengths, q_in, k_in, v_in, cos_q, min_q, plu_q, cos_k, min_k, plu_k,
    q_out, k_out, v_out, mixed_out, lse_out, *, rows, head_scale,
):
    step = pl.program_id(1)
    length = lengths[0]

    @pl.when(step == 0)
    def _():
        k_out[...] = turn_block(k_in[0], cos_k[...], min_k[...], plu_k[...], ROT // 2).astype(
            jnp.bfloat16
        )
        v_out[...] = v_in[0].astype(jnp.bfloat16)

    queries = (
        turn_block(q_in[0], cos_q[...], min_q[...], plu_q[...], ROT // 2) * head_scale
    ).astype(jnp.bfloat16)
    q_out[...] = queries

    def one_block(at, carried, diagonal):
        top, total, mixed = carried
        keys = k_out[pl.ds(at * rows, rows), :]
        values = v_out[pl.ds(at * rows, rows), :]
        scores = lax.dot_general(
            queries, keys, (((1,), (1,)), ((), ())), preferred_element_type=jnp.float32
        )
        places = lax.broadcasted_iota(jnp.int32, (rows, rows), 1)
        kept = places < length - at * rows
        if diagonal:
            kept = kept & (places <= lax.broadcasted_iota(jnp.int32, (rows, rows), 0))
        scores = jnp.where(kept, scores, masked_score)
        new_top = jnp.maximum(top, jnp.max(scores, axis=1, keepdims=True))
        shrink = jnp.exp(top - new_top)
        exponent = jnp.exp(scores - new_top)
        total = total * shrink + jnp.sum(exponent, axis=1, keepdims=True)
        mixed = mixed * shrink + lax.dot_general(
            exponent.astype(jnp.bfloat16),
            values,
            (((1,), (0,)), ((), ())),
            preferred_element_type=jnp.float32,
        )
        return (new_top, total, mixed)

    start = (
        jnp.full((rows, 1), masked_score, jnp.float32),
        jnp.zeros((rows, 1), jnp.float32),
        jnp.zeros((rows, HD), jnp.float32),
    )
    carried = lax.fori_loop(0, step, lambda at, c: one_block(at, c, False), start)
    top, total, mixed = one_block(step, carried, True)
    mixed_out[...] = (mixed / total).astype(jnp.bfloat16)
    lse_out[0] = top + jnp.log(total)


def backward_kernel(
    lengths, q_in, k_in, v_in, grad_in, mixed_in, lse_in, cosine, minus, plus,
    grads_out, key_sum, value_sum, *, rows, steps, head_scale,
):
    step = pl.program_id(1)
    length = lengths[0]

    @pl.when(step == 0)
    def _():
        key_sum[...] = jnp.zeros_like(key_sum)
        value_sum[...] = jnp.zeros_like(value_sum)

    queries = q_in[...]
    grads = grad_in[...]
    centre = jnp.sum(
        grads.astype(jnp.float32) * mixed_in[...].astype(jnp.float32), axis=1, keepdims=True
    )
    log_sum = lse_in[0]

    def one_block(at, grad_q, diagonal):
        span = pl.ds(at * rows, rows)
        keys = k_in[span, :]
        values = v_in[span, :]
        scores = lax.dot_general(
            queries, keys, (((1,), (1,)), ((), ())), preferred_element_type=jnp.float32
        )
        places = lax.broadcasted_iota(jnp.int32, (rows, rows), 1)
        kept = places < length - at * rows
        if diagonal:
            kept = kept & (places <= lax.broadcasted_iota(jnp.int32, (rows, rows), 0))
        weights = jnp.exp(jnp.where(kept, scores, masked_score) - log_sum)
        grad_w = lax.dot_general(
            grads, values, (((1,), (1,)), ((), ())), preferred_element_type=jnp.float32
        )
        grad_s = (weights * (grad_w - centre)).astype(jnp.bfloat16)
        key_sum[span, :] += lax.dot_general(
            grad_s, queries, (((0,), (0,)), ((), ())), preferred_element_type=jnp.float32
        )
        value_sum[span, :] += lax.dot_general(
            weights.astype(jnp.bfloat16),
            grads,
            (((0,), (0,)), ((), ())),
            preferred_element_type=jnp.float32,
        )
        return grad_q + lax.dot_general(
            grad_s, keys, (((1,), (0,)), ((), ())), preferred_element_type=jnp.float32
        )

    grad_q = lax.fori_loop(
        0, step, lambda at, c: one_block(at, c, False), jnp.zeros((rows, HD), jnp.float32)
    )
    grad_q = one_block(step, grad_q, True)
    here = pl.ds(step * rows, rows)
    grads_out[0, here, :] = (
        turn_block(grad_q, cosine[here, :], -minus[here, :], -plus[here, :], ROT // 2) * head_scale
    ).astype(jnp.bfloat16)

    @pl.when(step == steps - 1)
    def _():
        grads_out[1] = turn_block(
            key_sum[...], cosine[...], -minus[...], -plus[...], ROT // 2
        ).astype(jnp.bfloat16)
        grads_out[2] = value_sum[...].astype(jnp.bfloat16)


def attend_forward(projected, lengths, tables):
    _, span, width = projected.shape
    heads = width // HD
    rows = min(512, span)
    steps = span // rows
    low = jax.ShapeDtypeStruct((span, width), jnp.bfloat16)
    row_table = pl.BlockSpec((rows, LANES), lambda h, i, n: (i, 0))
    all_table = pl.BlockSpec((span, LANES), lambda h, i, n: (0, 0))
    row_block = pl.BlockSpec((rows, HD), lambda h, i, n: (i, h))
    all_block = pl.BlockSpec((span, HD), lambda h, i, n: (0, h))
    return pl.pallas_call(
        partial(forward_kernel, rows=rows, head_scale=HD ** (-0.5)),
        grid_spec=pltpu.PrefetchScalarGridSpec(
            num_scalar_prefetch=1,
            grid=(heads, steps),
            in_specs=[
                pl.BlockSpec((1, rows, HD), lambda h, i, n: (0, i, h)),
                pl.BlockSpec((1, span, HD), lambda h, i, n: (1, 0, h)),
                pl.BlockSpec((1, span, HD), lambda h, i, n: (2, 0, h)),
                row_table, row_table, row_table, all_table, all_table, all_table,
            ],
            out_specs=[
                row_block, all_block, all_block, row_block,
                pl.BlockSpec((1, rows, 1), lambda h, i, n: (h, i, 0)),
            ],
        ),
        out_shape=[low, low, low, low, jax.ShapeDtypeStruct((heads, span, 1), jnp.float32)],
        compiler_params=pltpu.CompilerParams(vmem_limit_bytes=48 * 1024 * 1024),
        name="attend_forward",
    )(lengths, projected, projected, projected, *tables, *tables)


def attend_backward(lengths, queries, keys, values, grad_mixed, mixed, lse, tables):
    span, width = queries.shape
    heads = width // HD
    rows = min(512, span)
    steps = span // rows
    all_table = pl.BlockSpec((span, LANES), lambda h, i, n: (0, 0))
    row_block = pl.BlockSpec((rows, HD), lambda h, i, n: (i, h))
    all_block = pl.BlockSpec((span, HD), lambda h, i, n: (0, h))
    return pl.pallas_call(
        partial(backward_kernel, rows=rows, steps=steps, head_scale=HD ** (-0.5)),
        grid_spec=pltpu.PrefetchScalarGridSpec(
            num_scalar_prefetch=1,
            grid=(heads, steps),
            in_specs=[
                row_block, all_block, all_block, row_block, row_block,
                pl.BlockSpec((1, rows, 1), lambda h, i, n: (h, i, 0)),
                all_table, all_table, all_table,
            ],
            out_specs=pl.BlockSpec((3, span, HD), lambda h, i, n: (0, 0, h)),
            scratch_shapes=[pltpu.VMEM((span, HD), jnp.float32)] * 2,
        ),
        out_shape=jax.ShapeDtypeStruct((3, span, width), jnp.bfloat16),
        compiler_params=pltpu.CompilerParams(vmem_limit_bytes=48 * 1024 * 1024),
        name="attend_backward",
    )(lengths, queries, keys, values, grad_mixed, mixed, lse, *tables)


def after(value, *others):
    return lax.optimization_barrier((value, *others))[0]


def tie(values, others):
    return lax.optimization_barrier((*values, *others))[: len(values)]


def xor_sum(vector, axis):
    size = lax.axis_size(axis)
    bit = 1
    while bit < size:
        vector = vector + lax.ppermute(vector, axis, [(i, i ^ bit) for i in range(size)])
        bit *= 2
    return vector


def widen_kernel(side, own, other, out):
    out[...] = jnp.where(pl.program_id(0) == side[0], own[...], other[...]).astype(jnp.float32)


def widen(own, other, side):
    rows, columns = own.shape
    step = math.gcd(rows, (512 * 1024) // columns)
    count = rows // step

    def held(half, at, used):
        return (jnp.where(half == used, at, jnp.where(half < used, 0, count - 1)), 0)

    return pl.pallas_call(
        widen_kernel,
        grid_spec=pltpu.PrefetchScalarGridSpec(
            num_scalar_prefetch=1,
            grid=(2, count),
            in_specs=[
                pl.BlockSpec((step, columns), lambda half, at, side: held(half, at, side[0])),
                pl.BlockSpec((step, columns), lambda half, at, side: held(half, at, 1 - side[0])),
            ],
            out_specs=pl.BlockSpec((step, columns), lambda half, at, side: (half * count + at, 0)),
        ),
        out_shape=jax.ShapeDtypeStruct((2 * rows, columns), jnp.float32),
        name="widen",
    )(jnp.reshape(side, (1,)).astype(jnp.int32), own, other)


def cube_sum(array, gate_of):
    size = lax.axis_size("dp")
    index = lax.axis_index("dp")
    bits = [1 << k for k in range(size.bit_length() - 1)]

    def exchange(value, bit):
        got = lax.ppermute(value, "dp", [(i, i ^ bit) for i in range(size)])
        return after(got, *gate_of())

    def halve(value, bit):
        half = value.shape[0] // 2
        side = (index // bit) % 2
        kept = lax.dynamic_slice_in_dim(value, side * half, half, 0)
        sent = lax.dynamic_slice_in_dim(value, (1 - side) * half, half, 0)
        got = exchange(sent, bit)
        return (kept.astype(jnp.float32) + got.astype(jnp.float32)).astype(value.dtype)

    def restore(value, bit):
        got = exchange(value, bit)
        upper = (index // bit) % 2 == 1
        return (jnp.where(upper, got, value), jnp.where(upper, value, got))

    array = halve(array, bits[0])
    yield (array,)
    middle = array.shape[0] // 2
    parts = [array[:middle], array[middle:]]
    orders = [bits[1:], bits[2:] + bits[1:2]]
    levels = range(len(bits) - 1)
    for level in levels:
        parts = [halve(part, order[level]) for part, order in zip(parts, orders)]
        yield tuple(parts)
    for level in reversed(levels):
        parts = [
            jnp.concatenate(restore(part, order[level]), axis=0)
            for part, order in zip(parts, orders)
        ]
        yield tuple(parts)
    own = jnp.concatenate(parts, axis=0)
    yield (widen(own, exchange(own, bits[0]), index % 2),)


class Sums:
    def __init__(self):
        self.running = {}
        self.totals = {}
        self.gate = ()

    def add(self, name, array):
        self.running[name] = cube_sum(array, lambda: self.gate)

    def step(self, *names, gate=()):
        moved = []
        self.gate = gate
        for name in names:
            latest = next(self.running[name], None) if name in self.running else ()
            if latest == ():
                continue
            if latest is None:
                del self.running[name]
            else:
                self.totals[name] = latest[0]
                moved += latest
        return moved

    def finish(self):
        while self.running:
            done = [total for total in self.totals.values() if total.dtype == jnp.float32]
            self.step(*self.running, gate=tuple(done))
        return self.totals


def on_device(
    tokens,
    lengths,
    cotangent,
    first_gain,
    first_shift,
    second_gain,
    second_shift,
    attend_weight,
    attend_bias,
    merge_weight,
    merge_bias,
    expand_weight,
    expand_bias,
    contract_weight,
    contract_bias,
):
    ring = lax.axis_size("mp")
    place = lax.axis_index("mp")
    rows_here, width = tokens.shape
    group_rows = rows_here * ring
    local_width = attend_weight.shape[2]
    f32, bf16 = jnp.float32, jnp.bfloat16
    dot = partial(jnp.einsum, preferred_element_type=f32)
    up = [(i, (i + 1) % ring) for i in range(ring)]
    down = [(i, (i - 1) % ring) for i in range(ring)]
    up_hops = ring // 2
    down_hops = ring - 1 - up_hops

    def owner_row(s):
        return ((place - s) % ring) * rows_here

    def gather_blocks(block):
        blocks = {0: block}
        for s in range(1, up_hops + 1):
            blocks[s] = lax.ppermute(blocks[s - 1], "mp", up)
        for s in range(1, down_hops + 1):
            blocks[ring - s] = lax.ppermute(blocks[(ring - s + 1) % ring], "mp", down)
        return blocks

    arrival = [0]
    for s in range(1, up_hops + 1):
        arrival += [s] + ([ring - s] if s <= down_hops else [])

    scatter_order = []
    for k in range(max(up_hops, down_hops)):
        if k < up_hops:
            scatter_order.append(("up", -(up_hops - k) % ring))
        if k < down_hops:
            scatter_order.append(("down", down_hops - k))

    def scatter_blocks(part_of, first_after=()):
        carried, arrived = {}, []
        for way, s in scatter_order:
            part = part_of(s)
            if way in carried:
                part = part + carried[way].astype(f32)
            part = part.astype(bf16)
            if way not in carried and first_after:
                part = after(part, *first_after)
            carried[way] = lax.ppermute(part, "mp", up if way == "up" else down)
            arrived.append(carried[way])
        total = part_of(0)
        for rows in carried.values():
            total = total + rows.astype(f32)
        return total, arrived

    def in_order(blocks):
        whole = jnp.zeros((group_rows, blocks[0].shape[1]), blocks[0].dtype)
        for s in arrival:
            whole = lax.dynamic_update_slice(whole, blocks[s], (owner_row(s), 0))
        return whole

    tables = rotary_tables(group_rows, ROT)

    token_blocks = gather_blocks(tokens)
    row_ids = place * rows_here + jnp.arange(rows_here)
    valid_rows = row_ids < lengths[0]
    grad_out = jnp.where(valid_rows[:, None], cotangent, jnp.zeros_like(cotangent))
    grad_blocks = gather_blocks(after(grad_out, token_blocks[up_hops]))

    projected = jnp.zeros((3, group_rows, local_width), f32)
    ones, twos, acts, slopes = {}, {}, {}, {}
    for s in arrival:
        hat, _ = standardize(token_blocks[s].astype(f32))
        ones[s] = (hat * first_gain + first_shift).astype(bf16)
        twos[s] = (hat * second_gain + second_shift).astype(bf16)
        part = dot("td,cde->cte", ones[s], attend_weight) + attend_bias[:, None, :]
        projected = lax.dynamic_update_slice(projected, part, (0, owner_row(s), 0))
        two = after(twos[s], token_blocks[up_hops]) if s == ring - 1 else twos[s]
        hidden = dot("td,df->tf", two, expand_weight) + expand_bias
        spread = 0.5 * (1.0 + lax.erf(hidden * (0.5**0.5)))
        bell = jnp.exp(-0.5 * hidden * hidden) * 0.3989422804014327
        acts[s] = (hidden * spread).astype(bf16)
        slopes[s] = (spread + hidden * bell).astype(bf16)

    projected = after(projected, *acts.values())
    queries, keys, values, mixed, lse = attend_forward(projected, lengths, tables)

    grad_blocks[0] = after(grad_blocks[0], grad_blocks[1], grad_blocks[ring - 1])
    hidden_grads = {}
    grad_mixed = jnp.zeros((group_rows, local_width), bf16)
    for s in arrival:
        block = grad_blocks[s]
        if s == ring - 1:
            block = after(block, grad_blocks[up_hops])
        grad_act = dot("td,fd->tf", block, contract_weight)
        hidden_grads[s] = (grad_act * slopes[s].astype(f32)).astype(bf16)
        rows = dot("td,fd->tf", block, merge_weight).astype(bf16)
        grad_mixed = lax.dynamic_update_slice(grad_mixed, rows, (owner_row(s), 0))

    def branch_part(s):
        mixed_rows = lax.dynamic_slice(mixed, (owner_row(s), 0), (rows_here, local_width))
        return dot("tf,fd->td", mixed_rows, merge_weight) + dot(
            "tf,fd->td", acts[s], contract_weight
        )

    branches, arrived = scatter_blocks(branch_part, (grad_blocks[up_hops],))
    layer_output = (tokens.astype(f32) + branches + merge_bias + contract_bias).astype(bf16)

    sums = Sums()
    full_grad = in_order(grad_blocks)
    full_hidden_grad = in_order(hidden_grads)
    contract_weight_grad = dot("tf,td->fd", in_order(acts), full_grad).astype(bf16)
    sums.add("contract", contract_weight_grad)

    (full_two,) = tie((in_order(twos),), (contract_weight_grad,))
    expand_weight_grad = dot("td,tf->df", full_two, full_hidden_grad).astype(bf16)
    moved = sums.step("contract", gate=(expand_weight_grad,))
    sums.add("expand", expand_weight_grad)

    (mixed_here,) = tie((mixed,), (expand_weight_grad, *moved))
    merge_weight_grad = dot("tf,td->fd", mixed_here, full_grad).astype(bf16)
    moved = sums.step("expand", gate=(merge_weight_grad,))
    sums.add("merge", merge_weight_grad)

    grad_projected = attend_backward(
        lengths,
        queries,
        keys,
        values,
        after(grad_mixed, merge_weight_grad, *moved),
        mixed,
        lse,
        tables,
    )
    moved = sums.step("contract", "merge", gate=(grad_projected,)) + arrived[:2]
    later_steps = [
        ("expand",),
        ("contract", "expand", "merge", "attend"),
        ("contract", "expand", "attend"),
        ("contract", "merge", "attend"),
        ("expand", "contract", "merge", "attend"),
    ]

    def next_step(made):
        return sums.step(*later_steps.pop(0), gate=(made,)) if later_steps else []

    grads_here, full_one = tie((grad_projected, in_order(ones)), moved)
    attend_weight_grad = dot("td,cte->cde", full_one, grads_here).astype(bf16)
    attend_weight_grad = attend_weight_grad.reshape(3 * width, local_width)
    moved = next_step(attend_weight_grad) + [attend_weight_grad]
    sums.add("attend", attend_weight_grad)

    vectors = []

    def normed_part(s):
        grads_rows = lax.dynamic_slice(
            grad_projected, (0, owner_row(s), 0), (3, rows_here, local_width)
        )
        grads_rows, hidden_rows = tie((grads_rows, hidden_grads[s]), moved)
        grad_one = dot("cte,cde->td", grads_rows, attend_weight)
        grad_two = dot("tf,df->td", hidden_rows, expand_weight)
        hat, _ = standardize(token_blocks[s].astype(f32))
        vectors.append(
            jnp.stack(
                [
                    jnp.sum(grad_one * hat, axis=0),
                    jnp.sum(grad_one, axis=0),
                    jnp.sum(grad_two * hat, axis=0),
                    jnp.sum(grad_two, axis=0),
                ]
            )
        )
        part = grad_one * first_gain + grad_two * second_gain
        moved[:] = next_step(part) + [part]
        return part

    weighted, _ = scatter_blocks(normed_part)
    hat, inverse = standardize(tokens.astype(f32))
    input_term = (
        weighted
        - jnp.mean(weighted, axis=-1, keepdims=True)
        - hat * jnp.mean(weighted * hat, axis=-1, keepdims=True)
    ) * inverse
    tokens_grad = (grad_out.astype(f32) + input_term).astype(bf16)

    summed = jnp.concatenate(
        [
            sum(vectors).reshape(-1),
            jnp.sum(grad_out, axis=0, dtype=f32),
            jnp.sum(grad_projected, axis=1, dtype=f32).reshape(-1),
            jnp.sum(full_hidden_grad, axis=0, dtype=f32),
        ]
    )
    summed = xor_sum(summed, "dp")
    heads_at = 5 * width
    first_gain_grad, first_shift_grad, second_gain_grad, second_shift_grad, bias_total = xor_sum(
        summed[:heads_at], "mp"
    ).reshape(5, width)
    biases = summed[heads_at:]
    attend_bias_grad = biases[: 3 * local_width].reshape(3, local_width)
    expand_bias_grad = biases[3 * local_width :]
    totals = sums.finish()
    return (
        layer_output,
        tokens_grad,
        first_gain_grad,
        first_shift_grad,
        second_gain_grad,
        second_shift_grad,
        totals["attend"].reshape(attend_weight.shape),
        attend_bias_grad,
        totals["merge"],
        bias_total,
        totals["expand"],
        expand_bias_grad,
        totals["contract"],
        bias_total,
    )


def solution(mesh):
    rows = P(("dp", "mp"), None)
    columns, row_split = P(None, "mp"), P("mp", None)
    return jax.shard_map(
        on_device,
        mesh=mesh,
        in_specs=(
            rows,
            P("dp"),
            rows,
            P(),
            P(),
            P(),
            P(),
            P(None, None, "mp"),
            columns,
            row_split,
            P(),
            columns,
            P("mp"),
            row_split,
            P(),
        ),
        out_specs=(
            rows,
            rows,
            P(),
            P(),
            P(),
            P(),
            P(None, None, "mp"),
            columns,
            row_split,
            P(),
            columns,
            P("mp"),
            row_split,
            P(),
        ),
        check_vma=False,
    )
```

```python
import math
from functools import partial

import jax
import jax.numpy as jnp
from jax import lax
from jax.experimental import pallas as pl
from jax.experimental.pallas import tpu as pltpu
from jax.sharding import PartitionSpec as P

HD = 256
ROT = 64
LANES = 128

norm_eps = 1e-05
masked_score = -1e30


def standardize(inputs):
    average = jnp.mean(inputs, axis=-1, keepdims=True)
    centred = inputs - average
    variance = jnp.mean(centred * centred, axis=-1, keepdims=True)
    inverse = lax.rsqrt(variance + norm_eps)
    return (centred * inverse, inverse)


def rotary_tables(length, rotated):
    halfway = rotated // 2
    channel = jnp.arange(halfway).astype(jnp.float32)
    frequency = 1.0 / 10000.0 ** (channel * 2.0 / rotated)
    positions = jnp.arange(length).astype(jnp.float32)
    angles = positions[:, None] * frequency[None, :]
    cosine, sine = jnp.cos(angles), jnp.sin(angles)
    rest = LANES - rotated
    ones, zeros = jnp.ones((length, rest), jnp.float32), jnp.zeros((length, rest), jnp.float32)
    none = jnp.zeros_like(sine)
    return (
        jnp.concatenate([cosine, cosine, ones], axis=1),
        jnp.concatenate([-sine, none, zeros], axis=1),
        jnp.concatenate([none, sine, zeros], axis=1),
    )


def turn_block(block, cosine, minus, plus, halfway):
    lead = block[:, :LANES]
    after = pltpu.roll(lead, LANES - halfway, 1)
    before = pltpu.roll(lead, halfway, 1)
    turned = lead * cosine + after * minus + before * plus
    return jnp.concatenate([turned, block[:, LANES:]], axis=1)


def forward_kernel(
    lengths, q_in, k_in, v_in, cos_q, min_q, plu_q, cos_k, min_k, plu_k,
    q_out, k_out, v_out, mixed_out, lse_out, *, rows, head_scale,
):
    step = pl.program_id(1)
    length = lengths[0]

    @pl.when(step == 0)
    def _():
        k_out[...] = turn_block(k_in[0], cos_k[...], min_k[...], plu_k[...], ROT // 2).astype(
            jnp.bfloat16
        )
        v_out[...] = v_in[0].astype(jnp.bfloat16)

    queries = (
        turn_block(q_in[0], cos_q[...], min_q[...], plu_q[...], ROT // 2) * head_scale
    ).astype(jnp.bfloat16)
    q_out[...] = queries

    def one_block(at, carried, diagonal):
        top, total, mixed = carried
        keys = k_out[pl.ds(at * rows, rows), :]
        values = v_out[pl.ds(at * rows, rows), :]
        scores = lax.dot_general(
            queries, keys, (((1,), (1,)), ((), ())), preferred_element_type=jnp.float32
        )
        places = lax.broadcasted_iota(jnp.int32, (rows, rows), 1)
        kept = places < length - at * rows
        if diagonal:
            kept = kept & (places <= lax.broadcasted_iota(jnp.int32, (rows, rows), 0))
        scores = jnp.where(kept, scores, masked_score)
        new_top = jnp.maximum(top, jnp.max(scores, axis=1, keepdims=True))
        shrink = jnp.exp(top - new_top)
        exponent = jnp.exp(scores - new_top)
        total = total * shrink + jnp.sum(exponent, axis=1, keepdims=True)
        mixed = mixed * shrink + lax.dot_general(
            exponent.astype(jnp.bfloat16),
            values,
            (((1,), (0,)), ((), ())),
            preferred_element_type=jnp.float32,
        )
        return (new_top, total, mixed)

    start = (
        jnp.full((rows, 1), masked_score, jnp.float32),
        jnp.zeros((rows, 1), jnp.float32),
        jnp.zeros((rows, HD), jnp.float32),
    )
    carried = lax.fori_loop(0, step, lambda at, c: one_block(at, c, False), start)
    top, total, mixed = one_block(step, carried, True)
    mixed_out[...] = (mixed / total).astype(jnp.bfloat16)
    lse_out[0] = top + jnp.log(total)


def backward_kernel(
    lengths, q_in, k_in, v_in, grad_in, mixed_in, lse_in, cosine, minus, plus,
    grads_out, key_sum, value_sum, *, rows, steps, head_scale,
):
    step = pl.program_id(1)
    length = lengths[0]

    @pl.when(step == 0)
    def _():
        key_sum[...] = jnp.zeros_like(key_sum)
        value_sum[...] = jnp.zeros_like(value_sum)

    queries = q_in[...]
    grads = grad_in[...]
    centre = jnp.sum(
        grads.astype(jnp.float32) * mixed_in[...].astype(jnp.float32), axis=1, keepdims=True
    )
    log_sum = lse_in[0]

    def one_block(at, grad_q, diagonal):
        span = pl.ds(at * rows, rows)
        keys = k_in[span, :]
        values = v_in[span, :]
        scores = lax.dot_general(
            queries, keys, (((1,), (1,)), ((), ())), preferred_element_type=jnp.float32
        )
        places = lax.broadcasted_iota(jnp.int32, (rows, rows), 1)
        kept = places < length - at * rows
        if diagonal:
            kept = kept & (places <= lax.broadcasted_iota(jnp.int32, (rows, rows), 0))
        weights = jnp.exp(jnp.where(kept, scores, masked_score) - log_sum)
        grad_w = lax.dot_general(
            grads, values, (((1,), (1,)), ((), ())), preferred_element_type=jnp.float32
        )
        grad_s = (weights * (grad_w - centre)).astype(jnp.bfloat16)
        key_sum[span, :] += lax.dot_general(
            grad_s, queries, (((0,), (0,)), ((), ())), preferred_element_type=jnp.float32
        )
        value_sum[span, :] += lax.dot_general(
            weights.astype(jnp.bfloat16),
            grads,
            (((0,), (0,)), ((), ())),
            preferred_element_type=jnp.float32,
        )
        return grad_q + lax.dot_general(
            grad_s, keys, (((1,), (0,)), ((), ())), preferred_element_type=jnp.float32
        )

    grad_q = lax.fori_loop(
        0, step, lambda at, c: one_block(at, c, False), jnp.zeros((rows, HD), jnp.float32)
    )
    grad_q = one_block(step, grad_q, True)
    here = pl.ds(step * rows, rows)
    grads_out[0, here, :] = (
        turn_block(grad_q, cosine[here, :], -minus[here, :], -plus[here, :], ROT // 2) * head_scale
    ).astype(jnp.bfloat16)

    @pl.when(step == steps - 1)
    def _():
        grads_out[1] = turn_block(
            key_sum[...], cosine[...], -minus[...], -plus[...], ROT // 2
        ).astype(jnp.bfloat16)
        grads_out[2] = value_sum[...].astype(jnp.bfloat16)


def attend_forward(projected, lengths, tables):
    _, span, width = projected.shape
    heads = width // HD
    rows = min(512, span)
    steps = span // rows
    low = jax.ShapeDtypeStruct((span, width), jnp.bfloat16)
    row_table = pl.BlockSpec((rows, LANES), lambda h, i, n: (i, 0))
    all_table = pl.BlockSpec((span, LANES), lambda h, i, n: (0, 0))
    row_block = pl.BlockSpec((rows, HD), lambda h, i, n: (i, h))
    all_block = pl.BlockSpec((span, HD), lambda h, i, n: (0, h))
    return pl.pallas_call(
        partial(forward_kernel, rows=rows, head_scale=HD ** (-0.5)),
        grid_spec=pltpu.PrefetchScalarGridSpec(
            num_scalar_prefetch=1,
            grid=(heads, steps),
            in_specs=[
                pl.BlockSpec((1, rows, HD), lambda h, i, n: (0, i, h)),
                pl.BlockSpec((1, span, HD), lambda h, i, n: (1, 0, h)),
                pl.BlockSpec((1, span, HD), lambda h, i, n: (2, 0, h)),
                row_table, row_table, row_table, all_table, all_table, all_table,
            ],
            out_specs=[
                row_block, all_block, all_block, row_block,
                pl.BlockSpec((1, rows, 1), lambda h, i, n: (h, i, 0)),
            ],
        ),
        out_shape=[low, low, low, low, jax.ShapeDtypeStruct((heads, span, 1), jnp.float32)],
        compiler_params=pltpu.CompilerParams(vmem_limit_bytes=48 * 1024 * 1024),
        name="attend_forward",
    )(lengths, projected, projected, projected, *tables, *tables)


def attend_backward(lengths, queries, keys, values, grad_mixed, mixed, lse, tables):
    span, width = queries.shape
    heads = width // HD
    rows = min(512, span)
    steps = span // rows
    all_table = pl.BlockSpec((span, LANES), lambda h, i, n: (0, 0))
    row_block = pl.BlockSpec((rows, HD), lambda h, i, n: (i, h))
    all_block = pl.BlockSpec((span, HD), lambda h, i, n: (0, h))
    return pl.pallas_call(
        partial(backward_kernel, rows=rows, steps=steps, head_scale=HD ** (-0.5)),
        grid_spec=pltpu.PrefetchScalarGridSpec(
            num_scalar_prefetch=1,
            grid=(heads, steps),
            in_specs=[
                row_block, all_block, all_block, row_block, row_block,
                pl.BlockSpec((1, rows, 1), lambda h, i, n: (h, i, 0)),
                all_table, all_table, all_table,
            ],
            out_specs=pl.BlockSpec((3, span, HD), lambda h, i, n: (0, 0, h)),
            scratch_shapes=[pltpu.VMEM((span, HD), jnp.float32)] * 2,
        ),
        out_shape=jax.ShapeDtypeStruct((3, span, width), jnp.bfloat16),
        compiler_params=pltpu.CompilerParams(vmem_limit_bytes=48 * 1024 * 1024),
        name="attend_backward",
    )(lengths, queries, keys, values, grad_mixed, mixed, lse, *tables)


def after(value, *others):
    return lax.optimization_barrier((value, *others))[0]


def tie(values, others):
    return lax.optimization_barrier((*values, *others))[: len(values)]


def xor_sum(vector, axis):
    size = lax.axis_size(axis)
    bit = 1
    while bit < size:
        vector = vector + lax.ppermute(vector, axis, [(i, i ^ bit) for i in range(size)])
        bit *= 2
    return vector


def widen_kernel(side, own, other, out):
    out[...] = jnp.where(pl.program_id(0) == side[0], own[...], other[...]).astype(jnp.float32)


def widen(own, other, side):
    rows, columns = own.shape
    step = math.gcd(rows, (512 * 1024) // columns)
    count = rows // step

    def held(half, at, used):
        return (jnp.where(half == used, at, jnp.where(half < used, 0, count - 1)), 0)

    return pl.pallas_call(
        widen_kernel,
        grid_spec=pltpu.PrefetchScalarGridSpec(
            num_scalar_prefetch=1,
            grid=(2, count),
            in_specs=[
                pl.BlockSpec((step, columns), lambda half, at, side: held(half, at, side[0])),
                pl.BlockSpec((step, columns), lambda half, at, side: held(half, at, 1 - side[0])),
            ],
            out_specs=pl.BlockSpec((step, columns), lambda half, at, side: (half * count + at, 0)),
        ),
        out_shape=jax.ShapeDtypeStruct((2 * rows, columns), jnp.float32),
        name="widen",
    )(jnp.reshape(side, (1,)).astype(jnp.int32), own, other)


def cube_sum(array, gate_of):
    size = lax.axis_size("dp")
    index = lax.axis_index("dp")
    bits = [1 << k for k in range(size.bit_length() - 1)]

    def exchange(value, bit):
        got = lax.ppermute(value, "dp", [(i, i ^ bit) for i in range(size)])
        return after(got, *gate_of())

    def halve(value, bit):
        half = value.shape[0] // 2
        side = (index // bit) % 2
        kept = lax.dynamic_slice_in_dim(value, side * half, half, 0)
        sent = lax.dynamic_slice_in_dim(value, (1 - side) * half, half, 0)
        got = exchange(sent, bit)
        return (kept.astype(jnp.float32) + got.astype(jnp.float32)).astype(value.dtype)

    def restore(value, bit):
        got = exchange(value, bit)
        upper = (index // bit) % 2 == 1
        return (jnp.where(upper, got, value), jnp.where(upper, value, got))

    array = halve(array, bits[0])
    yield (array,)
    middle = array.shape[0] // 2
    parts = [array[:middle], array[middle:]]
    orders = [bits[1:], bits[2:] + bits[1:2]]
    levels = range(len(bits) - 1)
    for level in levels:
        parts = [halve(part, order[level]) for part, order in zip(parts, orders)]
        yield tuple(parts)
    for level in reversed(levels):
        parts = [
            jnp.concatenate(restore(part, order[level]), axis=0)
            for part, order in zip(parts, orders)
        ]
        yield tuple(parts)
    own = jnp.concatenate(parts, axis=0)
    yield (widen(own, exchange(own, bits[0]), index % 2),)


class Sums:
    def __init__(self):
        self.running = {}
        self.totals = {}
        self.gate = ()

    def add(self, name, array):
        self.running[name] = cube_sum(array, lambda: self.gate)

    def step(self, *names, gate=()):
        moved = []
        self.gate = gate
        for name in names:
            latest = next(self.running[name], None) if name in self.running else ()
            if latest == ():
                continue
            if latest is None:
                del self.running[name]
            else:
                self.totals[name] = latest[0]
                moved += latest
        return moved

    def finish(self):
        while self.running:
            done = [total for total in self.totals.values() if total.dtype == jnp.float32]
            self.step(*self.running, gate=tuple(done))
        return self.totals


def on_device(
    tokens,
    lengths,
    cotangent,
    first_gain,
    first_shift,
    second_gain,
    second_shift,
    attend_weight,
    attend_bias,
    merge_weight,
    merge_bias,
    expand_weight,
    expand_bias,
    contract_weight,
    contract_bias,
):
    ring = lax.axis_size("mp")
    place = lax.axis_index("mp")
    rows_here, width = tokens.shape
    group_rows = rows_here * ring
    local_width = attend_weight.shape[2]
    f32, bf16 = jnp.float32, jnp.bfloat16
    dot = partial(jnp.einsum, preferred_element_type=f32)
    up = [(i, (i + 1) % ring) for i in range(ring)]
    down = [(i, (i - 1) % ring) for i in range(ring)]
    up_hops = ring // 2
    down_hops = ring - 1 - up_hops

    def owner_row(s):
        return ((place - s) % ring) * rows_here

    def gather_blocks(block):
        blocks = {0: block}
        for s in range(1, up_hops + 1):
            blocks[s] = lax.ppermute(blocks[s - 1], "mp", up)
        for s in range(1, down_hops + 1):
            blocks[ring - s] = lax.ppermute(blocks[(ring - s + 1) % ring], "mp", down)
        return blocks

    arrival = [0]
    for s in range(1, up_hops + 1):
        arrival += [s] + ([ring - s] if s <= down_hops else [])

    scatter_order = []
    for k in range(max(up_hops, down_hops)):
        if k < up_hops:
            scatter_order.append(("up", -(up_hops - k) % ring))
        if k < down_hops:
            scatter_order.append(("down", down_hops - k))

    def scatter_blocks(part_of, first_after=()):
        carried, arrived = {}, []
        for way, s in scatter_order:
            part = part_of(s)
            if way in carried:
                part = part + carried[way].astype(f32)
            part = part.astype(bf16)
            if way not in carried and first_after:
                part = after(part, *first_after)
            carried[way] = lax.ppermute(part, "mp", up if way == "up" else down)
            arrived.append(carried[way])
        total = part_of(0)
        for rows in carried.values():
            total = total + rows.astype(f32)
        return total, arrived

    def in_order(blocks):
        whole = jnp.zeros((group_rows, blocks[0].shape[1]), blocks[0].dtype)
        for s in arrival:
            whole = lax.dynamic_update_slice(whole, blocks[s], (owner_row(s), 0))
        return whole

    tables = rotary_tables(group_rows, ROT)

    token_blocks = gather_blocks(tokens)
    row_ids = place * rows_here + jnp.arange(rows_here)
    valid_rows = row_ids < lengths[0]
    grad_out = jnp.where(valid_rows[:, None], cotangent, jnp.zeros_like(cotangent))
    grad_blocks = gather_blocks(after(grad_out, token_blocks[up_hops]))

    projected = jnp.zeros((3, group_rows, local_width), f32)
    ones, twos, acts, slopes = {}, {}, {}, {}
    for s in arrival:
        hat, _ = standardize(token_blocks[s].astype(f32))
        ones[s] = (hat * first_gain + first_shift).astype(bf16)
        twos[s] = (hat * second_gain + second_shift).astype(bf16)
        part = dot("td,cde->cte", ones[s], attend_weight) + attend_bias[:, None, :]
        projected = lax.dynamic_update_slice(projected, part, (0, owner_row(s), 0))
        two = after(twos[s], token_blocks[up_hops]) if s == ring - 1 else twos[s]
        hidden = dot("td,df->tf", two, expand_weight) + expand_bias
        spread = 0.5 * (1.0 + lax.erf(hidden * (0.5**0.5)))
        bell = jnp.exp(-0.5 * hidden * hidden) * 0.3989422804014327
        acts[s] = (hidden * spread).astype(bf16)
        slopes[s] = (spread + hidden * bell).astype(bf16)

    projected = after(projected, *acts.values())
    queries, keys, values, mixed, lse = attend_forward(projected, lengths, tables)

    grad_blocks[0] = after(grad_blocks[0], grad_blocks[1], grad_blocks[ring - 1])
    hidden_grads = {}
    grad_mixed = jnp.zeros((group_rows, local_width), bf16)
    for s in arrival:
        block = grad_blocks[s]
        if s == ring - 1:
            block = after(block, grad_blocks[up_hops])
        grad_act = dot("td,fd->tf", block, contract_weight)
        hidden_grads[s] = (grad_act * slopes[s].astype(f32)).astype(bf16)
        rows = dot("td,fd->tf", block, merge_weight).astype(bf16)
        grad_mixed = lax.dynamic_update_slice(grad_mixed, rows, (owner_row(s), 0))

    def branch_part(s):
        mixed_rows = lax.dynamic_slice(mixed, (owner_row(s), 0), (rows_here, local_width))
        return dot("tf,fd->td", mixed_rows, merge_weight) + dot(
            "tf,fd->td", acts[s], contract_weight
        )

    branches, arrived = scatter_blocks(branch_part, (grad_blocks[up_hops],))
    layer_output = (tokens.astype(f32) + branches + merge_bias + contract_bias).astype(bf16)

    sums = Sums()
    full_grad = in_order(grad_blocks)
    full_hidden_grad = in_order(hidden_grads)
    contract_weight_grad = dot("tf,td->fd", in_order(acts), full_grad).astype(bf16)
    sums.add("contract", contract_weight_grad)

    moved = sums.step("contract", gate=(full_hidden_grad,))
    (full_two,) = tie((in_order(twos),), (contract_weight_grad, *moved))
    expand_weight_grad = dot("td,tf->df", full_two, full_hidden_grad).astype(bf16)
    moved = sums.step("contract", gate=(expand_weight_grad,))
    sums.add("expand", expand_weight_grad)

    (mixed_here,) = tie((mixed,), (expand_weight_grad, *moved))
    merge_weight_grad = dot("tf,td->fd", mixed_here, full_grad).astype(bf16)
    moved = sums.step("expand", gate=(merge_weight_grad,))
    sums.add("merge", merge_weight_grad)

    grad_projected = attend_backward(
        lengths,
        queries,
        keys,
        values,
        after(grad_mixed, merge_weight_grad, *moved),
        mixed,
        lse,
        tables,
    )
    moved = sums.step("expand", "contract", "merge", gate=(grad_projected,)) + arrived[:2]
    later_steps = [
        ("contract", "expand"),
        ("contract", "expand", "merge", "attend"),
        ("contract", "expand", "attend"),
        ("expand", "attend", "merge"),
        ("attend", "merge"),
    ]

    def next_step(made):
        return sums.step(*later_steps.pop(0), gate=(made,)) if later_steps else []

    grads_here, full_one = tie((grad_projected, in_order(ones)), moved)
    attend_weight_grad = dot("td,cte->cde", full_one, grads_here).astype(bf16)
    attend_weight_grad = attend_weight_grad.reshape(3 * width, local_width)
    moved = next_step(attend_weight_grad) + [attend_weight_grad]
    sums.add("attend", attend_weight_grad)

    vectors = []

    def normed_part(s):
        grads_rows = lax.dynamic_slice(
            grad_projected, (0, owner_row(s), 0), (3, rows_here, local_width)
        )
        grads_rows, hidden_rows = tie((grads_rows, hidden_grads[s]), moved)
        grad_one = dot("cte,cde->td", grads_rows, attend_weight)
        grad_two = dot("tf,df->td", hidden_rows, expand_weight)
        hat, _ = standardize(token_blocks[s].astype(f32))
        vectors.append(
            jnp.stack(
                [
                    jnp.sum(grad_one * hat, axis=0),
                    jnp.sum(grad_one, axis=0),
                    jnp.sum(grad_two * hat, axis=0),
                    jnp.sum(grad_two, axis=0),
                ]
            )
        )
        part = grad_one * first_gain + grad_two * second_gain
        moved[:] = next_step(part) + [part]
        return part

    weighted, _ = scatter_blocks(normed_part)
    hat, inverse = standardize(tokens.astype(f32))
    input_term = (
        weighted
        - jnp.mean(weighted, axis=-1, keepdims=True)
        - hat * jnp.mean(weighted * hat, axis=-1, keepdims=True)
    ) * inverse
    tokens_grad = (grad_out.astype(f32) + input_term).astype(bf16)

    summed = jnp.concatenate(
        [
            sum(vectors).reshape(-1),
            jnp.sum(grad_out, axis=0, dtype=f32),
            jnp.sum(grad_projected, axis=1, dtype=f32).reshape(-1),
            jnp.sum(full_hidden_grad, axis=0, dtype=f32),
        ]
    )
    summed = xor_sum(summed, "dp")
    heads_at = 5 * width
    first_gain_grad, first_shift_grad, second_gain_grad, second_shift_grad, bias_total = xor_sum(
        summed[:heads_at], "mp"
    ).reshape(5, width)
    biases = summed[heads_at:]
    attend_bias_grad = biases[: 3 * local_width].reshape(3, local_width)
    expand_bias_grad = biases[3 * local_width :]
    totals = sums.finish()
    return (
        layer_output,
        tokens_grad,
        first_gain_grad,
        first_shift_grad,
        second_gain_grad,
        second_shift_grad,
        totals["attend"].reshape(attend_weight.shape),
        attend_bias_grad,
        totals["merge"],
        bias_total,
        totals["expand"],
        expand_bias_grad,
        totals["contract"],
        bias_total,
    )


def solution(mesh):
    rows = P(("dp", "mp"), None)
    columns, row_split = P(None, "mp"), P("mp", None)
    return jax.shard_map(
        on_device,
        mesh=mesh,
        in_specs=(
            rows,
            P("dp"),
            rows,
            P(),
            P(),
            P(),
            P(),
            P(None, None, "mp"),
            columns,
            row_split,
            P(),
            columns,
            P("mp"),
            row_split,
            P(),
        ),
        out_specs=(
            rows,
            rows,
            P(),
            P(),
            P(),
            P(),
            P(None, None, "mp"),
            columns,
            row_split,
            P(),
            columns,
            P("mp"),
            row_split,
            P(),
        ),
        check_vma=False,
    )
```
